32 devices in a mesh: obj: 4 (over z), plane: 4 (over y, core), tile: 2 (over x).
Axes of the slice: x: 2, y: 2, z: 4, core: 2. Of those that a mesh axis runs over, the one named last changes fastest.
Arguments:
- tokens: bfloat16 [8, 3, 32, 32, 1024], P('obj', None, 'plane', 'tile'), may hold values from -6 to 6
- gout: bfloat16 [8, 3, 128, 128, 128], P('obj', None, 'plane', 'tile'), may hold values from -6 to 6
- deconv_weight: bfloat16 [1024, 2048], replicated, may hold values from -0.1875 to 0.1875
- deconv_bias: float32 [128], replicated, may hold values from -4 to 4
- conv_kernels: bfloat16 [2, 1152, 128], replicated, may hold values from -0.1875 to 0.1875
- conv_biases: float32 [2, 128], replicated, may hold values from -4 to 4
Outputs:
- d_tokens: bfloat16 [8, 3, 32, 32, 1024], P('obj', None, 'plane', 'tile')
- d_deconv_weight: float32 [1024, 2048], P(('obj', 'plane', 'tile'))
- d_deconv_bias: float32 [128], replicated
- d_conv_kernels: float32 [2, 1152, 128], replicated
- d_conv_biases: float32 [2, 128], replicated
The draws below stay inside these ranges and needn't reach their ends.
All inputs are finite; a program needn't handle non-finite values.
Results may differ from the reference program's by a relative error of at most 0.01.
Values may be sent and summed in bfloat16 or wider, within the bound.
No kernel may reach another device: no remote copies, remote signals or barrier semaphores. Data moves between devices by JAX's collectives and lax.ppermute only.
A program may use at most 192 MiB of HBM per device.

```python
import jax
import jax.numpy as jnp
from jax import lax

D = 1024
C = 128
LAYERS = 2
NOBJ = 8
TSIDE = 32
SIDE = 128


def levels(stream_key, shape, split, low, high):
    def one(position, shards_of):
        steps = jax.random.uniform(jax.random.fold_in(jax.random.fold_in(stream_key, 6), position), (shards_of,), jnp.float32, low / len(split), high / len(split))
        return jnp.repeat(jnp.exp(steps), shape[position] // shards_of).reshape((-1,) + (1,) * (len(shape) - position - 1))

    gain = one(*split[0])
    for cut in split[1:]:
        gain = gain * one(*cut)
    return gain


def noise(rng, dims, scale, bound, cuts=(), held_as=jnp.bfloat16):
    result = scale * jax.random.normal(rng, dims, jnp.float32)
    if cuts:
        result = result * levels(rng, dims, cuts, -0.22, 0.18)
    return jnp.clip(result, -bound, bound).astype(held_as)


def setup_inputs(seed: int = 0) -> dict:
    splits = jax.random.split(jax.random.key(seed), 7)
    tokens = noise(splits[0], (NOBJ, 3, TSIDE, TSIDE, D), 1.0, 6.0, ((0, 4), (2, 4), (3, 2)))
    gout = noise(splits[1], (NOBJ, 3, SIDE, SIDE, C), 1.0, 6.0, ((0, 4), (2, 4), (3, 2)))
    deconv_weight = noise(splits[2], (D, 16 * C), D ** -0.5, 0.1875)
    deconv_bias = noise(splits[3], (C,), 1.0, 4.0, (), jnp.float32)
    conv_kernels = noise(splits[4], (LAYERS, 9 * C, C), (9 * C) ** -0.5, 0.1875)
    conv_biases = noise(splits[5], (LAYERS, C), 0.7, 4.0, (), jnp.float32)
    return dict(tokens=tokens, gout=gout, deconv_weight=deconv_weight, deconv_bias=deconv_bias, conv_kernels=conv_kernels, conv_biases=conv_biases)


def columns(padded, height, breadth, flipped):
    pieces = []
    for tap_y in range(3):
        for tap_x in range(3):
            shift_y = 2 - tap_y if flipped else tap_y
            shift_x = 2 - tap_x if flipped else tap_x
            pieces.append(padded[..., shift_y:shift_y + height, shift_x:shift_x + breadth, :])
    return jnp.concatenate(pieces, axis=-1)

def convolve(padded, kernel, height, breadth, flipped):
    gathered = columns(padded, height, breadth, flipped)
    products = jnp.dot(gathered.reshape(-1, gathered.shape[-1]), kernel, preferred_element_type=jnp.float32)
    return products.reshape(padded.shape[:-3] + (height, breadth, kernel.shape[1]))

def upsample(tokens_here, weight, offsets):
    planes, tok_rows, tok_cols, fan_width = tokens_here.shape
    products = jnp.dot(tokens_here.reshape(-1, fan_width), weight, preferred_element_type=jnp.float32)
    products = products.reshape(planes, tok_rows, tok_cols, 4, 4, -1).transpose(0, 1, 3, 2, 4, 5)
    return products.reshape(planes, 4 * tok_rows, 4 * tok_cols, -1) + offsets

def tap_layout(gradient):
    planes, height, breadth, channels = gradient.shape
    blocks = gradient.reshape(planes, height // 4, 4, breadth // 4, 4, channels).transpose(0, 1, 3, 2, 4, 5)
    return blocks.reshape(-1, 16 * channels)

def contexts(row_sum, col_sum, extent):
    row_mean = row_sum / extent
    col_mean = col_sum / extent
    row_ctx = jnp.stack([row_mean[1], row_mean[0], col_mean[0]])
    col_ctx = jnp.stack([row_mean[2], col_mean[2], col_mean[1]])
    return (row_ctx, col_ctx)

def adjoint_contexts(row_sum, col_sum, extent):
    row_adjoint = jnp.stack([row_sum[1], row_sum[0], col_sum[0]])
    col_adjoint = jnp.stack([row_sum[2], col_sum[2], col_sum[1]])
    return (row_adjoint / extent, col_adjoint / extent)

def flip_kernel(kernel):
    channels = kernel.shape[1]
    return kernel.reshape(9, channels, channels).transpose(0, 2, 1).reshape(9 * channels, channels)

def one_object(tokens_here, grad_out, weight, offsets, kernels, kernel_bias):
    hidden = upsample(tokens_here, weight, offsets)
    planes, height, breadth, channels = hidden.shape
    extent = height
    stored = []
    for layer_index in range(kernels.shape[0]):
        row_ctx, col_ctx = contexts(lax.optimization_barrier(jnp.sum(hidden, 2)), lax.optimization_barrier(jnp.sum(hidden, 1)), extent)
        preact = hidden + row_ctx[:, :, None, :] + col_ctx[:, None, :, :]
        activated = jax.nn.silu(preact).astype(jnp.bfloat16)
        padded = jnp.pad(activated, ((0, 0), (1, 1), (1, 1), (0, 0)))
        kernel = kernels[layer_index]
        conv_out = lax.map(lambda single: convolve(single, kernel, height, breadth, False), padded)
        hidden = hidden + conv_out + kernel_bias[layer_index]
        stored.append((preact, padded))
    gradient = grad_out.astype(jnp.float32)
    kernel_grads = []
    bias_grads = []
    for layer_index in reversed(range(kernels.shape[0])):
        preact, padded = stored[layer_index]
        grad_bf = gradient.astype(jnp.bfloat16)
        bias_grads.insert(0, lax.optimization_barrier(jnp.sum(gradient, (0, 1, 2))))
        grad_pad = jnp.pad(grad_bf, ((0, 0), (1, 1), (1, 1), (0, 0)))
        flipped = flip_kernel(kernels[layer_index])
        act_grad = lax.map(lambda single: convolve(single, flipped, height, breadth, True), grad_pad)

        def plane_kernel_grad(object_pair):
            gathered = columns(object_pair[0], height, breadth, False)
            return lax.dot_general(gathered.reshape(-1, gathered.shape[-1]), object_pair[1].reshape(-1, channels), (((0,), (0,)), ((), ())), preferred_element_type=jnp.float32)
        kernel_grads.insert(0, lax.optimization_barrier(jnp.sum(lax.map(plane_kernel_grad, (padded, grad_bf)), 0)))
        sigmoid_pre = jax.nn.sigmoid(preact)
        pre_grad = act_grad * sigmoid_pre * (1.0 + preact * (1.0 - sigmoid_pre))
        row_adjoint, col_adjoint = adjoint_contexts(lax.optimization_barrier(jnp.sum(pre_grad, 2)), lax.optimization_barrier(jnp.sum(pre_grad, 1)), extent)
        gradient = gradient + pre_grad + row_adjoint[:, :, None, :] + col_adjoint[:, None, :, :]
    grad_bf = gradient.astype(jnp.bfloat16)
    tap_grads = tap_layout(grad_bf)
    tok_grad = lax.dot_general(tap_grads, weight, (((1,), (1,)), ((), ())), preferred_element_type=jnp.float32)
    tok_grad = tok_grad.astype(jnp.bfloat16).reshape(tokens_here.shape)
    tok_flat = tokens_here.reshape(-1, tokens_here.shape[-1])
    weight_grad = lax.dot_general(tok_flat, tap_grads, (((0,), (0,)), ((), ())), preferred_element_type=jnp.float32)
    return (tok_grad, weight_grad, lax.optimization_barrier(jnp.sum(gradient, (0, 1, 2))), jnp.stack(kernel_grads), jnp.stack(bias_grads))

def reference(tokens, gout, deconv_weight, deconv_bias, conv_kernels, conv_biases):
    results = lax.map(lambda object_pair: one_object(object_pair[0], object_pair[1], deconv_weight, deconv_bias, conv_kernels, conv_biases), (tokens, gout))
    return (results[0], lax.optimization_barrier(jnp.sum(results[1], 0)), lax.optimization_barrier(jnp.sum(results[2], 0)), lax.optimization_barrier(jnp.sum(results[3], 0)), lax.optimization_barrier(jnp.sum(results[4], 0)))
```

```python
import functools

import jax
import jax.numpy as jnp
from jax import lax
from jax.experimental import pallas as pl
from jax.experimental.pallas import tpu as pltpu
from jax.sharding import PartitionSpec as P

BANDS = ("plane", "tile")
EVERY = ("obj", "plane", "tile")
CONV_DIMS = ("NHWC", "HWIO", "NHWC")
BF = jnp.bfloat16
F32 = jnp.float32


def shifted(array, axis, step):
    size = lax.axis_size(axis)
    pairs = [(i, i + step) for i in range(size) if 0 <= i + step < size]
    return lax.ppermute(array, axis, pairs)


def grow_dim(tok, grad, axis, dim, tok_rim, grad_rim):
    planes, lanes = tok.shape[0], grad.shape[-1]

    def cut(array, rim, last):
        length = array.shape[dim]
        start = length - rim if last else 0
        return lax.slice_in_dim(array, start, start + rim, axis=dim)

    def pack(last):
        parts = [cut(tok, tok_rim, last), cut(grad, grad_rim, last)]
        return jnp.concatenate([part.reshape(planes, -1, lanes) for part in parts], 1)

    def unpack(packed):
        shapes = [cut(tok, tok_rim, False).shape, cut(grad, grad_rim, False).shape]
        rows = shapes[0][1] * shapes[0][2] * shapes[0][3] // lanes
        return packed[:, :rows].reshape(shapes[0]), packed[:, rows:].reshape(shapes[1])

    before = unpack(shifted(pack(True), axis, 1))
    after = unpack(shifted(pack(False), axis, -1))
    return [
        jnp.concatenate([low, mid, high], axis=dim)
        for low, mid, high in zip(before, (tok, grad), after)
    ]


def band_sums(rows, cols):
    height = rows.shape[1]

    def joined(own, other, axis, step):
        upper = (lax.axis_index(axis) & step) != 0
        return jnp.where(
            upper, jnp.concatenate([other, own], 1), jnp.concatenate([own, other], 1)
        )

    rows, cols = rows.astype(BF), cols.astype(BF)
    for axis in ("tile", "plane"):
        size, step = lax.axis_size(axis), 1
        while step < size:
            height = rows.shape[1]
            other = lax.ppermute(
                jnp.concatenate([rows, cols], 1), axis, [(i, i ^ step) for i in range(size)]
            )
            other_rows, other_cols = other[:, :height], other[:, height:]
            if axis == "tile":
                rows = (rows.astype(F32) + other_rows.astype(F32)).astype(BF)
                cols = joined(cols, other_cols, axis, step)
            else:
                rows = joined(rows, other_rows, axis, step)
                cols = (cols.astype(F32) + other_cols.astype(F32)).astype(BF)
            step *= 2
    return rows.astype(F32), cols.astype(F32)


def spread(row_sum, col_sum, extent, ring, row_start, col_start, height, breadth):
    planes, _, channels = row_sum.shape
    rows = row_sum.reshape(planes // 3, 3, extent, channels) / extent
    cols = col_sum.reshape(planes // 3, 3, extent, channels) / extent
    row_ctx = jnp.stack([rows[:, 1], rows[:, 0], cols[:, 0]], 1)
    col_ctx = jnp.stack([rows[:, 2], cols[:, 2], cols[:, 1]], 1)

    def band(ctx, start, length):
        ctx = jnp.pad(ctx, ((0, 0), (0, 0), (ring, ring), (0, 0)))
        ctx = lax.dynamic_slice_in_dim(ctx, start, length + 2 * ring, 2)
        return ctx.reshape(planes, length + 2 * ring, channels)

    row_band = band(row_ctx, row_start, height)
    col_band = band(col_ctx, col_start, breadth)
    return row_band[:, :, None, :] + col_band[:, None, :, :]


def inside(ring, extent, row_start, col_start, height, breadth):
    row = row_start - ring + lax.iota(jnp.int32, height + 2 * ring)
    col = col_start - ring + lax.iota(jnp.int32, breadth + 2 * ring)
    row_ok = (row >= 0) & (row < extent)
    col_ok = (col >= 0) & (col < extent)
    return (row_ok[:, None] & col_ok[None, :])[None, :, :, None]


def conv(padded, kernel):
    return lax.conv_general_dilated(
        padded, kernel, (1, 1), "VALID", dimension_numbers=CONV_DIMS, preferred_element_type=F32
    )


def kernel_gradient(padded, grad):
    return lax.conv_general_dilated(
        padded,
        grad,
        (1, 1),
        "VALID",
        dimension_numbers=("CHWN", "IHWO", "HWNC"),
        preferred_element_type=F32,
    )


def trim(array, ring):
    return array[:, ring:-ring, ring:-ring, :]


def slope(pre):
    sig = jax.nn.sigmoid(pre)
    return sig * (1.0 + pre * (1.0 - sig))


def scattered(parts, axes):
    return jnp.sum(lax.all_to_all(parts, axes, 0, 0, tiled=True).astype(F32), 0)


def scatter_all(blocks, sizes):
    objs, bands = sizes
    blocks = blocks.astype(BF).reshape((objs, bands) + blocks.shape[1:])
    blocks = jnp.moveaxis(blocks, 1, 0)
    part = scattered(blocks, BANDS).astype(BF)
    return scattered(part, "obj")


def call(kernel, planes, ins, outs, scratch=(), flops=0):
    def spec(shape, shared):
        if shared:
            return pl.BlockSpec(shape, lambda p: (0,) * len(shape))
        return pl.BlockSpec((None,) + shape[1:], lambda p: (p,) + (0,) * (len(shape) - 1))

    moved = sum(a.size * a.dtype.itemsize for a, _ in ins)
    return pl.pallas_call(
        kernel,
        grid=(planes,),
        in_specs=[spec(a.shape, shared) for a, shared in ins],
        out_specs=[spec(shape, shared) for shape, _, shared in outs],
        out_shape=[jax.ShapeDtypeStruct(shape, dtype) for shape, dtype, _ in outs],
        scratch_shapes=list(scratch),
        compiler_params=pltpu.CompilerParams(
            dimension_semantics=("arbitrary",), vmem_limit_bytes=60 << 20
        ),
        cost_estimate=pl.CostEstimate(
            flops=flops * planes, bytes_accessed=2 * moved, transcendentals=0
        ),
    )(*[a for a, _ in ins])


def span(row, width, rows=1):
    return pl.ds(pl.multiple_of(row * width, 16), rows * width)


def span8(start, size):
    return pl.ds(pl.multiple_of(start, 8), size)


def loop(rows, body, carry=None, unroll=2):
    return lax.fori_loop(0, rows, body, carry, unroll=unroll)


def convolve_rows(src, base, kernel_ref, prod, rows_out, width, chunks, finish, carry):
    step = rows_out // chunks
    size = step * width

    def chunk(index, carry):
        start = base + index * step
        lhs = jnp.concatenate([src[span(start + dy, width, step), :] for dy in range(3)], 1)
        prod[pl.ds(8, size), :] = jnp.dot(lhs, kernel_ref[...], preferred_element_type=F32)
        channels = prod.shape[1] // 3

        def row(r, carry):
            view = prod.at[span8(r * width, width + 16), :]
            value = (
                view[7 : 7 + width, :channels]
                + view[8 : 8 + width, channels : 2 * channels]
                + view[9 : 9 + width, 2 * channels :]
            )
            return finish(index * step + r, value, carry)

        return loop(step, row, carry)

    return lax.fori_loop(0, chunks, chunk, carry)


def upsample_kernel(dims, tok_ref, ring_ref, weight_ref, raw_ref, sums_ref):
    tok_rows, tok_cols, up, height, breadth, width, channels = dims
    edge = (width - breadth) // 2
    cut = up * channels
    for a in range(up):
        weight = weight_ref[:, a * cut : (a + 1) * cut]
        prod = jnp.dot(tok_ref[...], weight, preferred_element_type=F32)
        rim = jnp.dot(ring_ref[...], weight, preferred_element_type=F32)
        for b in range(up):
            lanes = slice(b * channels, (b + 1) * channels)
            for i in range(tok_rows):
                at = (2 + up * i + a) * width + edge + b
                raw_ref[pl.ds(at, tok_cols, stride=up), :] = prod[
                    i * tok_cols : (i + 1) * tok_cols, lanes
                ]
            if a >= up - 2:
                at = (a - up + 2) * width + edge + b
                raw_ref[pl.ds(at, tok_cols, stride=up), :] = rim[:tok_cols, lanes]
            if a < 2:
                at = (2 + height + a) * width + edge + b
                raw_ref[pl.ds(at, tok_cols, stride=up), :] = rim[tok_cols : 2 * tok_cols, lanes]
            first = 0 if a >= up - 2 else 1
            row = up * first + a - up + 2
            count = tok_rows + 1 if a >= up - 2 or a < 2 else tok_rows
            for side in range(2):
                at = 2 * tok_cols + side * (tok_rows + 2) + first
                column = edge - up + b if side == 0 else edge + breadth + b
                if (b >= up - 2) if side == 0 else (b < 2):
                    raw_ref[pl.ds(row * width + column, count, stride=up * width), :] = rim[
                        at : at + count, lanes
                    ]

    def add(r, total):
        own = raw_ref[span8((r + 2) * width + edge, breadth), :]
        sums_ref[pl.ds(r, 1), :] = jnp.sum(own, 0, keepdims=True)
        return total + own

    sums_ref[pl.ds(height, breadth), :] = loop(height, add, jnp.zeros((breadth, channels), F32))


def forward_kernel(
    dims, raw_ref, row_ref, col_ref, rok_ref, cok_ref, kernel_ref,
    act_ref, slope_ref, next_ref, sums_ref, prod,
):
    height, breadth, width = dims
    edge = (width - breadth) // 2

    def activate(r, carry):
        pre = raw_ref[span(r, width), :] + row_ref[pl.ds(r, 1), :] + col_ref[...]
        sig = 0.5 * jnp.tanh(0.5 * pre) + 0.5
        ok = cok_ref[...] * rok_ref[pl.ds(r, 1), :] > 0.5
        act_ref[span(r, width), :] = jnp.where(ok, pre * sig, 0.0).astype(BF)
        slope_ref[span(r, width), :] = (sig * (1.0 + pre * (1.0 - sig))).astype(BF)
        return carry

    loop(height + 4, activate, 0)
    zero = jnp.zeros((breadth, sums_ref.shape[1]), F32)

    def finish(r, value, total):
        value = raw_ref[span(r + 1, width), :] + value
        next_ref[span(r, width), :] = value
        own = value[edge : edge + breadth]
        inner = (r >= 1) & (r <= height)

        @pl.when(inner)
        def _():
            sums_ref[pl.ds(r - 1, 1), :] = jnp.sum(own, 0, keepdims=True)

        return total + jnp.where(inner, own, 0.0)

    sums_ref[pl.ds(height, breadth), :] = convolve_rows(
        act_ref, 0, kernel_ref, prod, height + 2, width, 2, finish, zero
    )


def adjoint_kernel(
    dims, own_ref, above_ref, below_ref, left_ref, right_ref, kernel_ref, wide_ref, out_ref, prod
):
    height, breadth, width = dims
    edge = (width - breadth) // 2

    def place(r, center):
        row = [left_ref[span8(r * edge, edge), :], center, right_ref[span8(r * edge, edge), :]]
        wide_ref[span(r, width), :] = jnp.concatenate(row, 0).astype(BF)

    for r in range(2):
        place(r, above_ref[r * breadth : (r + 1) * breadth, :].astype(F32))
        place(r + 2 + height, below_ref[r * breadth : (r + 1) * breadth, :].astype(F32))

    def fill(r, carry):
        place(r + 2, own_ref[span(r, breadth), :].astype(F32))
        return carry

    loop(height, fill, 0)

    def finish(r, value, carry):
        out_ref[span(r, width), :] = value
        return carry

    convolve_rows(wide_ref, 0, kernel_ref, prod, height + 2, width, 2, finish, 0)


def context_kernel(dims, ring, side, start_ref, parts_ref, bias_ref, row_ref, col_ref, rows, cols):
    height, breadth, _ = dims
    bands, planes = parts_ref.shape[:2]
    extent = rows.shape[1] - 16
    down, across = extent // height, extent // breadth
    rows[...] = jnp.zeros(rows.shape, F32)
    cols[...] = jnp.zeros(cols.shape, F32)
    scale = 1.0 / extent
    for first in range(0, planes, 3):
        for q in range(3):
            part = lambda p, t, at, size: parts_ref[p * across + t, first + q, at : at + size, :].astype(F32)
            for p in range(down):
                pieces = [part(p, t, 0, height) for t in range(across)]
                rows[q, 8 + p * height : 8 + (p + 1) * height, :] = scale * sum(pieces)
            for t in range(across):
                pieces = [part(p, t, height, breadth) for p in range(down)]
                cols[q, 8 + t * breadth : 8 + (t + 1) * breadth, :] = scale * sum(pieces)
        row_at = span8(start_ref[0], height + 16)
        col_at = span8(start_ref[1], breadth + 16)
        for q, (ref, other) in enumerate(((rows, 1), (rows, 0), (cols, 0))):
            view = ref.at[other, row_at, :]
            row_ref[first + q] = view[8 - ring : 8 + height + ring, :] + 2.0 * bias_ref[...]
        for q, (ref, other) in enumerate(((rows, 2), (cols, 2), (cols, 1))):
            view = ref.at[other, col_at, :]
            col_ref[first + q] = view[8 - side : 8 + breadth + side, :] + bias_ref[...]


def middle_kernel(
    dims, hid_ref, adj_ref, grad_ref, row_ref, col_ref, rok_ref, cok_ref,
    act_ref, next_ref, sums_ref,
):
    height, breadth, width = dims
    edge = (width - breadth) // 2

    def one(r, total):
        pre = hid_ref[span(r, width), :] + row_ref[pl.ds(r, 1), :] + col_ref[...]
        sig = 0.5 * jnp.tanh(0.5 * pre) + 0.5
        ok = cok_ref[...] * rok_ref[pl.ds(r, 1), :] > 0.5
        act_ref[span(r, width), :] = jnp.where(ok, pre * sig, 0.0).astype(BF)
        dz = adj_ref[span(r, width), :] * (sig * (1.0 + pre * (1.0 - sig)))
        next_ref[span(r, width), :] = grad_ref[span(r + 1, width), :].astype(F32) + dz
        own = dz[edge : edge + breadth]
        inner = (r >= 1) & (r <= height)

        @pl.when(inner)
        def _():
            sums_ref[pl.ds(r - 1, 1), :] = jnp.sum(own, 0, keepdims=True)

        return total + jnp.where(inner, own, 0.0)

    sums_ref[pl.ds(height, breadth), :] = loop(height + 2, one, jnp.zeros((breadth, sums_ref.shape[1]), F32))


def backward_kernel(
    dims, part_ref, slope_ref, row_ref, col_ref, rok_ref, cok_ref, kernel_ref,
    grad_ref, next_ref, sums_ref, bias_ref, prod,
):
    height, breadth, width = dims
    edge = (width - breadth) // 2

    def full(r):
        return part_ref[span(r, width), :] + row_ref[pl.ds(r, 1), :] + col_ref[...]

    def round_row(r, carry):
        ok = cok_ref[...] * rok_ref[pl.ds(r, 1), :] > 0.5
        grad_ref[span(r, width), :] = jnp.where(ok, full(r), 0.0).astype(BF)
        return carry

    loop(height + 2, round_row, 0)
    zero = jnp.zeros((breadth, sums_ref.shape[1]), F32)

    def finish(r, value, carry):
        total, bias = carry
        dz = value * slope_ref[span(r + 2, width), :].astype(F32)
        own = dz[edge : edge + breadth]
        grad = full(r + 1)[edge : edge + breadth]
        sums_ref[pl.ds(r, 1), :] = jnp.sum(own, 0, keepdims=True)
        next_ref[pl.ds(pl.multiple_of(r * breadth, 16), breadth), :] = grad + own
        return total + own, bias + grad

    total, bias = convolve_rows(
        grad_ref, 0, kernel_ref, prod, height, width, 2, finish, (zero, zero)
    )
    sums_ref[pl.ds(height, breadth), :] = total
    bias_ref[...] = jnp.sum(bias, 0, keepdims=True)


def taps_kernel(dims, part_ref, row_ref, col_ref, tap_ref, bias_ref, full):
    height, breadth, up, channels = dims

    def one(r, total):
        at = pl.ds(pl.multiple_of(r * breadth, 16), breadth)
        value = part_ref[at, :] + row_ref[pl.ds(r, 1), :] + col_ref[...]
        full[at, :] = value
        return total + value

    total = loop(height, one, jnp.zeros(col_ref.shape, F32))
    bias_ref[...] = jnp.sum(total, 0, keepdims=True)
    tok_cols = breadth // up
    for i in range(height // up):
        for a in range(up):
            for b in range(up):
                piece = full[pl.ds((up * i + a) * breadth + b, tok_cols, stride=up), :]
                tap = a * up + b
                tap_ref[
                    i * tok_cols : (i + 1) * tok_cols, tap * channels : (tap + 1) * channels
                ] = piece.astype(BF)


def kernel_grad_kernel(dims, act_base, grad_base, act_ref, grad_ref, out_ref, wide, moved):
    height, breadth, width = dims
    edge = (width - breadth) // 2
    channels = act_ref.shape[1]
    column = lax.broadcasted_iota(jnp.int32, (width, channels), 0)
    ok = (column >= edge) & (column < edge + breadth)
    wide[pl.ds(0, 8), :] = jnp.zeros((8, channels), F32)
    wide[pl.ds(8 + height * width, 8), :] = jnp.zeros((8, channels), F32)

    def fill(r, carry):
        value = grad_ref[span(r + grad_base, width), :].astype(F32)
        wide[span8(r * width + 8, width), :] = jnp.where(ok, value, 0.0)
        return carry

    loop(height, fill, 0)

    def move(r, carry):
        view = wide.at[span8(r * width, width + 16), :]
        for dx in range(3):
            moved[span(r, width), dx * channels : (dx + 1) * channels] = view[
                9 - dx : 9 - dx + width, :
            ].astype(BF)
        return carry

    loop(height, move, 0)

    @pl.when(pl.program_id(0) == 0)
    def _():
        out_ref[...] = jnp.zeros(out_ref.shape, F32)

    chunks = 2
    step = height // chunks

    def chunk(index, carry):
        start = index * step
        lhs = jnp.concatenate(
            [act_ref[span(start + act_base + dy, width, step), :] for dy in range(3)], 1
        )
        out_ref[...] += lax.dot_general(
            lhs,
            moved[span(start, width, step), :],
            (((0,), (0,)), ((), ())),
            preferred_element_type=F32,
        )
        return carry

    lax.fori_loop(0, chunks, chunk, 0)


def plain_pass(tokens, gout, deconv_weight, deconv_bias, conv_kernels, conv_biases):
    objects, _, tok_rows, tok_cols, fan = tokens.shape
    _, _, height, breadth, channels = gout.shape
    planes = 3 * objects
    up = height // tok_rows
    extent = height * lax.axis_size("plane")
    row_start = lax.axis_index("plane") * height
    col_start = lax.axis_index("tile") * breadth
    place = (extent, row_start, col_start, height, breadth)
    ctx_place = (row_start, col_start, height, breadth)

    tok = tokens.reshape(planes, tok_rows, tok_cols, fan)
    grad_top = gout.reshape(planes, height, breadth, channels)
    tok_wide, grad_wide = grow_dim(tok, grad_top, "plane", 1, 1, 2)
    tok_wide, grad_wide = grow_dim(tok_wide, grad_wide, "tile", 2, 1, 2)

    taps = conv_kernels.reshape(2, 3, 3, channels, channels)
    back = taps[:, ::-1, ::-1].transpose(0, 1, 2, 4, 3)

    raw = jnp.dot(tok_wide.reshape(-1, fan), deconv_weight, preferred_element_type=F32)
    raw = raw.reshape(planes, tok_rows + 2, tok_cols + 2, up, up, channels)
    raw = raw.transpose(0, 1, 3, 2, 4, 5)
    raw = raw.reshape(planes, up * (tok_rows + 2), up * (tok_cols + 2), channels)
    raw = trim(raw, up - 2)

    own = trim(raw, 2)
    row0, col0 = band_sums(jnp.sum(own, 2), jnp.sum(own, 1))
    bias = deconv_bias
    pre0 = raw + bias + spread(
        row0 + extent * bias, col0 + extent * bias, extent, 2, *ctx_place
    )
    act0 = jnp.where(inside(2, *place), jax.nn.silu(pre0), 0.0).astype(BF)
    step0 = conv(act0, taps[0])

    own = trim(step0, 1)
    row1, col1 = band_sums(jnp.sum(own, 2), jnp.sum(own, 1))
    bias = deconv_bias + conv_biases[0]
    pre1 = trim(raw, 1) + step0 + bias + spread(
        row0 + row1 + extent * bias, col0 + col1 + extent * bias, extent, 1, *ctx_place
    )
    ok1 = inside(1, *place)
    act1 = jnp.where(ok1, jax.nn.silu(pre1), 0.0).astype(BF)

    dz1 = conv(grad_wide, back[1]) * slope(pre1)
    own = trim(dz1, 1)
    drow1, dcol1 = band_sums(jnp.sum(own, 2), jnp.sum(own, 1))
    kernel1 = kernel_gradient(act1, grad_top)
    cbias1 = jnp.sum(grad_top.astype(F32), (0, 1, 2))
    grad1 = trim(grad_wide, 1).astype(F32) + dz1 + spread(drow1, dcol1, extent, 1, *ctx_place)
    gb1 = jnp.where(ok1, grad1, 0.0).astype(BF)
    own1 = trim(grad1, 1)
    cbias0 = jnp.sum(own1, (0, 1, 2))

    dz0 = conv(gb1, back[0]) * slope(trim(pre0, 2))
    drow0, dcol0 = band_sums(jnp.sum(dz0, 2), jnp.sum(dz0, 1))
    kernel0 = kernel_gradient(trim(act0, 1), trim(gb1, 1))
    grad0 = own1 + dz0 + spread(drow0, dcol0, extent, 0, *ctx_place)
    bias_part = jnp.sum(grad0, (0, 1, 2))

    gb0 = grad0.astype(BF).reshape(planes, tok_rows, up, tok_cols, up, channels)
    tap_grads = gb0.transpose(0, 1, 3, 2, 4, 5).reshape(-1, up * up * channels)
    tok_grad = lax.dot_general(
        tap_grads, deconv_weight, (((1,), (1,)), ((), ())), preferred_element_type=F32
    )
    tok_grad = tok_grad.astype(BF).reshape(tokens.shape)
    weight_part = lax.dot_general(
        tok.reshape(-1, fan), tap_grads, (((0,), (0,)), ((), ())), preferred_element_type=F32
    )
    small = jnp.concatenate(
        [kernel0.reshape(-1, channels), kernel1.reshape(-1, channels)]
        + [v.reshape(1, channels) for v in (cbias0, cbias1, bias_part)],
        0,
    )
    bands = lax.axis_size("plane") * lax.axis_size("tile")
    total = lax.axis_size("obj") * bands
    weight_grad = scatter_all(
        weight_part.reshape(total, fan // total, -1), (lax.axis_size("obj"), bands)
    )
    return (tok_grad, weight_grad) + finish_small(small, conv_kernels.shape[1])


def edges(ring, extent, start, length, side, channels):
    place = lax.iota(jnp.int32, length + 2 * side) - side
    ok = (place >= -ring) & (place < length + ring)
    ok = ok & (start + place >= 0) & (start + place < extent)
    return jnp.broadcast_to(ok[:, None].astype(F32), (length + 2 * side, channels))


def sent_to_all(array, axes):
    copies = jnp.broadcast_to(array[None], (lax.axis_size(axes),) + array.shape)
    return lax.all_to_all(copies, axes, 0, 0, tiled=True)


def finish_small(small, per_kernel):
    rows, channels = small.shape
    bands = lax.axis_size("plane") * lax.axis_size("tile")
    piece = -(-rows // bands)
    piece += -piece % 16
    parts = jnp.pad(small, ((0, piece * bands - rows), (0, 0))).astype(BF)
    part = scattered(parts.reshape(bands, piece, channels), BANDS).astype(BF)
    part = jnp.sum(sent_to_all(part, "obj").astype(F32), 0).astype(BF)
    small = sent_to_all(part, BANDS).reshape(-1, channels).astype(F32)
    kernel_grads = small[: 2 * per_kernel].reshape(2, per_kernel, channels)
    cbias_grads = small[2 * per_kernel : 2 * per_kernel + 2]
    return (small[2 * per_kernel + 2], kernel_grads, cbias_grads)


def bits_of(size):
    steps = []
    while size > 1:
        size //= 2
        steps.append(size)
    return steps


def halved(parts, dim, axis, step):
    upper = ((lax.axis_index(axis) // step) % 2).astype(jnp.int32)
    size = lax.axis_size(axis)
    mine = lax.dynamic_slice_in_dim(parts, upper, 1, dim)
    theirs = lax.dynamic_slice_in_dim(parts, 1 - upper, 1, dim)
    other = lax.ppermute(theirs, axis, [(i, i ^ step) for i in range(size)])
    return (mine.astype(F32) + other.astype(F32)).astype(BF)


def scatter_weight(product, fan, columns):
    objs = lax.axis_size("obj")
    steps = [("plane", s) for s in bits_of(lax.axis_size("plane"))]
    steps += [("tile", s) for s in bits_of(lax.axis_size("tile"))]
    block = fan // (objs * 2 ** len(steps))
    shape = (objs,) + (2,) * len(steps) + (block, columns)
    parts = product.astype(BF).reshape(shape)
    order = list(range(len(steps)))
    near = order.index(len(bits_of(lax.axis_size("plane"))) - 1)
    parts = halved(parts, 1 + near, *steps[near])
    rest = [i for i in order if i != near]
    streams = [parts[: objs // 2], parts[objs // 2 :]]
    for one, two in zip(rest, reversed(rest)):
        streams[0] = halved(streams[0], 1 + one, *steps[one])
        streams[1] = halved(streams[1], 1 + two, *steps[two])
    parts = jnp.concatenate(streams, 0).reshape(objs, block, columns)
    return scattered(parts, "obj")


def kernel_pass(tokens, gout, deconv_weight, deconv_bias, conv_kernels, conv_biases):
    objects, _, tok_rows, tok_cols, fan = tokens.shape
    _, _, height, breadth, channels = gout.shape
    planes = 3 * objects
    up = height // tok_rows
    edge = 8
    width = breadth + 2 * edge
    extent = height * lax.axis_size("plane")
    row_start = lax.axis_index("plane") * height
    col_start = lax.axis_index("tile") * breadth
    dims = (height, breadth, width)

    tok = tokens.reshape(planes, tok_rows, tok_cols, fan)
    grad_top = gout.reshape(planes, height, breadth, channels)
    tok_above, tok_below = shifted(tok[:, -1:], "plane", 1), shifted(tok[:, :1], "plane", -1)
    above, below = shifted(grad_top[:, -2:], "plane", 1), shifted(grad_top[:, :2], "plane", -1)

    def column(parts, last, rim):
        cut = lambda part: part[:, :, -rim:] if last else part[:, :, :rim]
        return jnp.concatenate([cut(part) for part in parts], 1)

    tok_parts, grad_parts = (tok_above, tok, tok_below), (above, grad_top, below)
    tok_left = shifted(column(tok_parts, True, 1), "tile", 1)
    tok_right = shifted(column(tok_parts, False, 1), "tile", -1)
    left = shifted(column(grad_parts, True, 2), "tile", 1)
    right = shifted(column(grad_parts, False, 2), "tile", -1)
    flat_tok = lambda array: array.reshape(planes, -1, fan)
    ring = jnp.concatenate([flat_tok(a) for a in (tok_above, tok_below, tok_left, tok_right)], 1)
    ring = jnp.pad(ring, ((0, 0), (0, -ring.shape[1] % 16), (0, 0)))
    flat_grad = lambda array: array.reshape(planes, -1, channels)
    left = flat_grad(jnp.pad(left, ((0, 0), (0, 0), (edge - 2, 0), (0, 0))).astype(F32))
    right = flat_grad(jnp.pad(right, ((0, 0), (0, 0), (0, edge - 2), (0, 0))).astype(F32))

    taps = conv_kernels.reshape(2, 3, 3, channels, channels)
    side = 3 * channels
    ahead = taps[0].transpose(0, 2, 1, 3).reshape(side, side)
    back = taps[:, ::-1, ::-1].transpose(0, 1, 4, 2, 3).reshape(2, side, side)

    def oks(rim):
        return (
            edges(rim, extent, row_start, height, rim, channels),
            edges(rim, extent, col_start, breadth, edge, channels),
        )

    flat = lambda rows: (planes, rows * width, channels)
    sums = ((planes, height + breadth, channels), F32, False)
    one = ((planes, 1, channels), F32, False)
    prod = lambda rows: pltpu.VMEM((rows * width + 16, side), F32)
    conv_flops = lambda rows: 2 * rows * width * side * side
    starts = jnp.stack([row_start, col_start]).astype(jnp.int32)

    def contexts(parts, rim, pad, bias, beside=None):
        parts = sent_to_all(parts.astype(BF), BANDS)
        if beside is not None:
            parts, beside = lax.optimization_barrier((parts, beside))
        whole = lambda array: pl.BlockSpec(memory_space=pltpu.VMEM)
        shapes = [
            jax.ShapeDtypeStruct((planes, height + 2 * rim, channels), F32),
            jax.ShapeDtypeStruct((planes, breadth + 2 * pad, channels), F32),
        ]
        terms = pl.pallas_call(
            functools.partial(context_kernel, dims, rim, pad),
            in_specs=[pl.BlockSpec(memory_space=pltpu.SMEM), whole(parts), whole(bias)],
            out_specs=[whole(shape) for shape in shapes],
            out_shape=shapes,
            scratch_shapes=[pltpu.VMEM((3, extent + 16, channels), F32)] * 2,
            compiler_params=pltpu.CompilerParams(vmem_limit_bytes=60 << 20),
            cost_estimate=pl.CostEstimate(
                flops=4 * parts.size, bytes_accessed=2 * parts.size, transcendentals=0
            ),
        )(starts, parts, bias.reshape(1, channels))
        return tuple(terms) if beside is None else tuple(terms) + (beside,)

    raw, parts = call(
        functools.partial(
            upsample_kernel, (tok_rows, tok_cols, up, height, breadth, width, channels)
        ),
        planes,
        [(flat_tok(tok), False), (ring, False), (deconv_weight, True)],
        [(flat(height + 4), F32, False), sums],
        flops=2 * 192 * fan * up * up * channels,
    )
    row_ctx, col_ctx = contexts(parts, 2, edge, deconv_bias)
    grad_wide, adjoint = call(
        functools.partial(adjoint_kernel, dims),
        planes,
        [(flat_grad(a), False) for a in (grad_top, above, below)]
        + [(left, False), (right, False), (back[1], True)],
        [(flat(height + 4), BF, False), (flat(height + 2), F32, False)],
        [prod(height // 2 + 1)],
        conv_flops(height + 2),
    )
    row_ok2, col_ok2 = oks(2)
    act0, slope0, hidden, parts = call(
        functools.partial(forward_kernel, dims),
        planes,
        [(raw, False), (row_ctx, False), (col_ctx, False)]
        + [(row_ok2, True), (col_ok2, True), (ahead, True)],
        [(flat(height + 4), BF, False)] * 2 + [(flat(height + 2), F32, False), sums],
        [prod(height // 2 + 1)],
        conv_flops(height + 2),
    )
    row_ctx, col_ctx = contexts(parts, 1, edge, deconv_bias + conv_biases[0])
    row_ok1, col_ok1 = oks(1)
    act1, part1, parts = call(
        functools.partial(middle_kernel, dims),
        planes,
        [(hidden, False), (adjoint, False), (grad_wide, False)]
        + [(row_ctx, False), (col_ctx, False), (row_ok1, True), (col_ok1, True)],
        [(flat(height + 2), BF, False), (flat(height + 2), F32, False), sums],
    )

    def kernel_gradient_of(act, grad, act_base, grad_base):
        (result,) = call(
            functools.partial(kernel_grad_kernel, dims, act_base, grad_base),
            planes,
            [(act, False), (grad, False)],
            [((side, side), F32, True)],
            [
                pltpu.VMEM((height * width + 16, channels), F32),
                pltpu.VMEM((height * width, side), BF),
            ],
            2 * height * width * side * side,
        )
        result = result.reshape(3, channels, 3, channels).transpose(0, 2, 1, 3)
        return result.reshape(-1, channels)

    none = jnp.zeros((channels,), F32)
    kernel1 = kernel_gradient_of(act1, grad_wide, 0, 2)
    row_ctx, col_ctx, kernel1 = contexts(parts, 1, edge, none, kernel1)
    cbias1 = jnp.sum(grad_top.astype(F32), (0, 1, 2))
    gb1, part0, parts, cbias0 = call(
        functools.partial(backward_kernel, dims),
        planes,
        [(part1, False), (slope0, False), (row_ctx, False), (col_ctx, False)]
        + [(row_ok1, True), (col_ok1, True), (back[0], True)],
        [(flat(height + 2), BF, False), ((planes, height * breadth, channels), F32, False)]
        + [sums, one],
        [prod(height // 2)],
        conv_flops(height),
    )
    kernel0 = kernel_gradient_of(act0, gb1, 1, 1)
    row_ctx, col_ctx, kernel0 = contexts(parts, 0, 0, none, kernel0)
    tap_grads, bias_part = call(
        functools.partial(taps_kernel, (height, breadth, up, channels)),
        planes,
        [(part0, False), (row_ctx, False), (col_ctx, False)],
        [((planes, tok_rows * tok_cols, up * up * channels), BF, False), one],
        [pltpu.VMEM((height * breadth, channels), F32)],
    )
    tap_grads = tap_grads.reshape(-1, up * up * channels)
    product = lax.dot_general(
        tok.reshape(-1, fan), tap_grads, (((0,), (0,)), ((), ())), preferred_element_type=F32
    )
    weight_grad = scatter_weight(product, fan, up * up * channels)
    tok_grad = lax.dot_general(
        tap_grads, deconv_weight, (((1,), (1,)), ((), ())), preferred_element_type=F32
    )
    tok_grad = tok_grad.astype(BF).reshape(tokens.shape)
    small = jnp.concatenate(
        [kernel0, kernel1, jnp.sum(cbias0, 0), cbias1[None], jnp.sum(bias_part, 0)], 0
    )
    return (tok_grad, weight_grad) + finish_small(small, conv_kernels.shape[1])


def per_device(tokens, gout, deconv_weight, deconv_bias, conv_kernels, conv_biases):
    channels = gout.shape[-1]
    sizes = [lax.axis_size(axis) for axis in ("obj", "plane", "tile")]
    fits = gout.shape[3] % 16 == 0 and gout.shape[2] % 16 == 0 and channels % 128 == 0
    fits = fits and all(size & (size - 1) == 0 and size > 1 for size in sizes)
    run = kernel_pass if fits else plain_pass
    return run(tokens, gout, deconv_weight, deconv_bias, conv_kernels, conv_biases)


def solution(mesh):
    placed = (
        P("obj", None, "plane", "tile", None),
        P("obj", None, "plane", "tile", None),
        P(),
        P(),
        P(),
        P(),
    )
    return jax.shard_map(
        per_device,
        mesh=mesh,
        in_specs=placed,
        out_specs=(
            P("obj", None, "plane", "tile", None),
            P(EVERY, None),
            P(),
            P(),
            P(),
        ),
        check_vma=False,
    )
```

```python
import functools

import jax
import jax.numpy as jnp
from jax import lax
from jax.experimental import pallas as pl
from jax.experimental.pallas import tpu as pltpu
from jax.sharding import PartitionSpec as P

BANDS = ("plane", "tile")
EVERY = ("obj", "plane", "tile")
CONV_DIMS = ("NHWC", "HWIO", "NHWC")
BF = jnp.bfloat16
F32 = jnp.float32


def shifted(array, axis, step):
    size = lax.axis_size(axis)
    pairs = [(i, i + step) for i in range(size) if 0 <= i + step < size]
    return lax.ppermute(array, axis, pairs)


def grow_dim(tok, grad, axis, dim, tok_rim, grad_rim):
    planes, lanes = tok.shape[0], grad.shape[-1]

    def cut(array, rim, last):
        length = array.shape[dim]
        start = length - rim if last else 0
        return lax.slice_in_dim(array, start, start + rim, axis=dim)

    def pack(last):
        parts = [cut(tok, tok_rim, last), cut(grad, grad_rim, last)]
        return jnp.concatenate([part.reshape(planes, -1, lanes) for part in parts], 1)

    def unpack(packed):
        shapes = [cut(tok, tok_rim, False).shape, cut(grad, grad_rim, False).shape]
        rows = shapes[0][1] * shapes[0][2] * shapes[0][3] // lanes
        return packed[:, :rows].reshape(shapes[0]), packed[:, rows:].reshape(shapes[1])

    before = unpack(shifted(pack(True), axis, 1))
    after = unpack(shifted(pack(False), axis, -1))
    return [
        jnp.concatenate([low, mid, high], axis=dim)
        for low, mid, high in zip(before, (tok, grad), after)
    ]


def band_sums(rows, cols):
    height = rows.shape[1]

    def joined(own, other, axis, step):
        upper = (lax.axis_index(axis) & step) != 0
        return jnp.where(
            upper, jnp.concatenate([other, own], 1), jnp.concatenate([own, other], 1)
        )

    rows, cols = rows.astype(BF), cols.astype(BF)
    for axis in ("tile", "plane"):
        size, step = lax.axis_size(axis), 1
        while step < size:
            height = rows.shape[1]
            other = lax.ppermute(
                jnp.concatenate([rows, cols], 1), axis, [(i, i ^ step) for i in range(size)]
            )
            other_rows, other_cols = other[:, :height], other[:, height:]
            if axis == "tile":
                rows = (rows.astype(F32) + other_rows.astype(F32)).astype(BF)
                cols = joined(cols, other_cols, axis, step)
            else:
                rows = joined(rows, other_rows, axis, step)
                cols = (cols.astype(F32) + other_cols.astype(F32)).astype(BF)
            step *= 2
    return rows.astype(F32), cols.astype(F32)


def spread(row_sum, col_sum, extent, ring, row_start, col_start, height, breadth):
    planes, _, channels = row_sum.shape
    rows = row_sum.reshape(planes // 3, 3, extent, channels) / extent
    cols = col_sum.reshape(planes // 3, 3, extent, channels) / extent
    row_ctx = jnp.stack([rows[:, 1], rows[:, 0], cols[:, 0]], 1)
    col_ctx = jnp.stack([rows[:, 2], cols[:, 2], cols[:, 1]], 1)

    def band(ctx, start, length):
        ctx = jnp.pad(ctx, ((0, 0), (0, 0), (ring, ring), (0, 0)))
        ctx = lax.dynamic_slice_in_dim(ctx, start, length + 2 * ring, 2)
        return ctx.reshape(planes, length + 2 * ring, channels)

    row_band = band(row_ctx, row_start, height)
    col_band = band(col_ctx, col_start, breadth)
    return row_band[:, :, None, :] + col_band[:, None, :, :]


def inside(ring, extent, row_start, col_start, height, breadth):
    row = row_start - ring + lax.iota(jnp.int32, height + 2 * ring)
    col = col_start - ring + lax.iota(jnp.int32, breadth + 2 * ring)
    row_ok = (row >= 0) & (row < extent)
    col_ok = (col >= 0) & (col < extent)
    return (row_ok[:, None] & col_ok[None, :])[None, :, :, None]


def conv(padded, kernel):
    return lax.conv_general_dilated(
        padded, kernel, (1, 1), "VALID", dimension_numbers=CONV_DIMS, preferred_element_type=F32
    )


def kernel_gradient(padded, grad):
    return lax.conv_general_dilated(
        padded,
        grad,
        (1, 1),
        "VALID",
        dimension_numbers=("CHWN", "IHWO", "HWNC"),
        preferred_element_type=F32,
    )


def trim(array, ring):
    return array[:, ring:-ring, ring:-ring, :]


def slope(pre):
    sig = jax.nn.sigmoid(pre)
    return sig * (1.0 + pre * (1.0 - sig))


def scattered(parts, axes):
    return jnp.sum(lax.all_to_all(parts, axes, 0, 0, tiled=True).astype(F32), 0)


def scatter_all(blocks, sizes):
    objs, bands = sizes
    blocks = blocks.astype(BF).reshape((objs, bands) + blocks.shape[1:])
    blocks = jnp.moveaxis(blocks, 1, 0)
    part = scattered(blocks, BANDS).astype(BF)
    return scattered(part, "obj")


def call(kernel, planes, ins, outs, scratch=(), flops=0):
    def spec(shape, kind):
        rest = (0,) * (len(shape) - 1)
        if kind is True:
            return pl.BlockSpec(shape, lambda p: (0,) + rest)
        if kind == "copies":
            return pl.BlockSpec(
                (shape[0], None) + shape[2:], lambda p: (0, p) + (0,) * (len(shape) - 2)
            )
        if kind is False:
            return pl.BlockSpec((None,) + shape[1:], lambda p: (p,) + rest)
        first, count = kind
        if count < 0:
            return pl.BlockSpec((None,) + shape[1:], lambda p: (p + first,) + rest)
        return pl.BlockSpec(
            (None,) + shape[1:], lambda p: (jnp.clip(p - first, 0, count - 1),) + rest
        )

    moved = sum(a.size * a.dtype.itemsize for a, _ in ins)
    return pl.pallas_call(
        kernel,
        grid=(planes,),
        in_specs=[spec(a.shape, kind) for a, kind in ins],
        out_specs=[spec(shape, kind) for shape, _, kind in outs],
        out_shape=[jax.ShapeDtypeStruct(shape, dtype) for shape, dtype, _ in outs],
        scratch_shapes=list(scratch),
        compiler_params=pltpu.CompilerParams(
            dimension_semantics=("arbitrary",), vmem_limit_bytes=60 << 20
        ),
        cost_estimate=pl.CostEstimate(
            flops=flops * planes, bytes_accessed=2 * moved, transcendentals=0
        ),
    )(*[a for a, _ in ins])


def inside_limits(ring, extent, height, breadth, width):
    row_start = lax.axis_index("plane") * height
    col_start = lax.axis_index("tile") * breadth
    edge = (width - breadth) // 2
    column = lax.broadcasted_iota(jnp.int32, (width, 128), 0) - edge
    ok = (column >= -ring) & (column < breadth + ring)
    ok = ok & (col_start + column >= 0) & (col_start + column < extent)
    ones = jnp.where(ok, 1.0, 0.0)

    def limit(r):
        row = row_start + r - ring
        return jnp.where((row >= 0) & (row < extent), 0.5, 2.0)

    return ones, limit


def span(row, width, rows=1):
    return pl.ds(pl.multiple_of(row * width, 16), rows * width)


def span8(start, size):
    return pl.ds(pl.multiple_of(start, 8), size)


def loop(rows, body, carry=None, unroll=4):
    return lax.fori_loop(0, rows, body, carry, unroll=unroll)


def convolve_rows(
    src, base, kernel_ref, prod, rows_out, width, chunks, finish, carry, flipped=False
):
    step = rows_out // chunks
    size = step * width
    order = (2, 1, 0) if flipped else (0, 1, 2)

    def chunk(index, carry):
        start = base + index * step
        lhs = jnp.concatenate([src[span(start + dy, width, step), :] for dy in order], 1)
        prod[pl.ds(8, size), :] = jnp.dot(lhs, kernel_ref[...], preferred_element_type=F32)
        channels = prod.shape[1] // 3

        def row(r, carry):
            view = prod.at[span8(r * width, width + 16), :]
            first, _, last = order
            value = (
                view[7 + first : 7 + first + width, :channels]
                + view[8 : 8 + width, channels : 2 * channels]
                + view[7 + last : 7 + last + width, 2 * channels :]
            )
            return finish(index * step + r, value, carry)

        return loop(step, row, carry)

    return lax.fori_loop(0, chunks, chunk, carry)


def send_sums(sums, copies_ref):
    for copy in range(copies_ref.shape[0]):
        copies_ref[copy] = sums[...].astype(BF)


def place_row(rows, r, slot, center, left_ref, right_ref):
    side = left_ref.shape[0] // rows // 2
    at = span8((2 * r + slot) * side, side)
    return jnp.concatenate([left_ref[at, :], center, right_ref[at, :]], 0)


def place_rows(rows, breadth, slot, refs, put):
    own_ref, above_ref, below_ref, left_ref, right_ref = refs

    def one(r, ref, at):
        center = ref[at, :].astype(F32)
        put(r, place_row(rows, r, slot, center, left_ref, right_ref))

    for r in range(2):
        at = (2 * slot + r) * breadth
        one(r, above_ref, slice(at, at + breadth))
        one(rows - 2 + r, below_ref, slice(at, at + breadth))

    def inner(r, carry):
        one(r + 2, own_ref, span(r, breadth))
        return carry

    loop(rows - 4, inner, 0)


def upsample_kernel(
    dims, tok_ref, grad_ref, weight_ref,
    raw_ref, copies_ref, first_ref, last_ref, bias_ref, sums,
):
    tok_rows, tok_cols, up, height, breadth, channels = dims
    cut = up * channels
    for a in range(up):
        weight = weight_ref[:, a * cut : (a + 1) * cut]
        prod = jnp.dot(tok_ref[...], weight, preferred_element_type=F32)
        for b in range(up):
            for i in range(tok_rows):
                raw_ref[pl.ds((up * i + a) * breadth + b, tok_cols, stride=up), :] = prod[
                    i * tok_cols : (i + 1) * tok_cols, b * channels : (b + 1) * channels
                ]

    def add(r, total):
        own = raw_ref[span(r, breadth), :]
        sums[pl.ds(r, 1), :] = jnp.sum(own, 0, keepdims=True)
        total, bias = total
        return total + own, bias + grad_ref[span(r, breadth), :].astype(F32)

    zero = jnp.zeros((breadth, channels), F32)
    total, bias = loop(height, add, (zero, zero))
    sums[pl.ds(height, breadth), :] = total
    bias_ref[...] = jnp.sum(bias, 0, keepdims=True)
    send_sums(sums, copies_ref)
    rim = 2 * breadth
    tail = slice((height - 2) * breadth, height * breadth)
    for ref, at in ((first_ref, slice(0, rim)), (last_ref, tail)):
        ref[:rim, :] = grad_ref[at, :]
        ref[rim:, :] = raw_ref[at, :].astype(BF)


def forward_kernel(
    dims, extent, own_ref, above_ref, below_ref, left_ref, right_ref,
    row_ref, col_ref, kernel_ref,
    act_ref, slope_ref, next_ref, copies_ref, raw_ref, prod, sums_ref, mask,
):
    height, breadth, width = dims
    mask[...], limit = inside_limits(2, extent, height, breadth, width)
    edge = (width - breadth) // 2

    def activate(r, value):
        raw_ref[span(r, width), :] = value
        pre = value + row_ref[pl.ds(r, 1), :] + col_ref[...]
        sig = 0.5 * jnp.tanh(0.5 * pre) + 0.5
        ok = mask[...] > limit(r)
        act_ref[span(r, width), :] = jnp.where(ok, pre * sig, 0.0).astype(BF)
        slope_ref[span(r, width), :] = (sig * (1.0 + pre * (1.0 - sig))).astype(BF)

    refs = (own_ref, above_ref, below_ref, left_ref, right_ref)
    place_rows(height + 4, breadth, 1, refs, activate)
    zero = jnp.zeros((breadth, sums_ref.shape[1]), F32)

    def finish(r, value, total):
        value = raw_ref[span(r + 1, width), :] + value
        next_ref[span(r, width), :] = value.astype(BF)
        own = value[edge : edge + breadth]
        inner = (r >= 1) & (r <= height)

        @pl.when(inner)
        def _():
            sums_ref[pl.ds(r - 1, 1), :] = jnp.sum(own, 0, keepdims=True)

        return total + jnp.where(inner, own, 0.0)

    sums_ref[pl.ds(height, breadth), :] = convolve_rows(
        act_ref, 0, kernel_ref, prod, height + 2, width, 2, finish, zero
    )
    send_sums(sums_ref, copies_ref)


def adjoint_kernel(
    dims, own_ref, above_ref, below_ref, left_ref, right_ref, kernel_ref, wide_ref, out_ref, prod
):
    height, breadth, width = dims

    def put(r, row):
        wide_ref[span(r, width), :] = row.astype(BF)

    refs = (own_ref, above_ref, below_ref, left_ref, right_ref)
    place_rows(height + 4, breadth, 0, refs, put)

    def finish(r, value, carry):
        out_ref[span(r, width), :] = value.astype(BF)
        return carry

    convolve_rows(wide_ref, 0, kernel_ref, prod, height + 2, width, 2, finish, 0, True)


def context_kernel(dims, ring, side, parts_ref, bias_ref, row_ref, col_ref, rows, cols):
    height, breadth, _ = dims
    bands, planes = parts_ref.shape[:2]
    extent = rows.shape[1] - 16
    down, across = extent // height, extent // breadth
    rows[...] = jnp.zeros(rows.shape, F32)
    cols[...] = jnp.zeros(cols.shape, F32)
    scale = 1.0 / extent
    for first in range(0, planes, 3):
        for q in range(3):
            part = lambda p, t, at, size: parts_ref[p * across + t, first + q, at : at + size, :].astype(F32)
            for p in range(down):
                pieces = [part(p, t, 0, height) for t in range(across)]
                rows[q, 8 + p * height : 8 + (p + 1) * height, :] = scale * sum(pieces)
            for t in range(across):
                pieces = [part(p, t, height, breadth) for p in range(down)]
                cols[q, 8 + t * breadth : 8 + (t + 1) * breadth, :] = scale * sum(pieces)
        row_at = span8(lax.axis_index("plane") * height, height + 16)
        col_at = span8(lax.axis_index("tile") * breadth, breadth + 16)
        for q, (ref, other) in enumerate(((rows, 1), (rows, 0), (cols, 0))):
            view = ref.at[other, row_at, :]
            row_ref[first + q] = view[8 - ring : 8 + height + ring, :] + 2.0 * bias_ref[...]
        for q, (ref, other) in enumerate(((rows, 2), (cols, 2), (cols, 1))):
            view = ref.at[other, col_at, :]
            col_ref[first + q] = view[8 - side : 8 + breadth + side, :] + bias_ref[...]


def middle_kernel(
    dims, extent, half, hid_ref, adj_low, adj_high, grad_low, grad_high,
    row_ref, col_ref, act_ref, next_ref, copies_ref, sums_ref, mask,
):
    height, breadth, width = dims
    mask[...], limit = inside_limits(1, extent, height, breadth, width)
    low = pl.program_id(0) < half
    edge = (width - breadth) // 2

    def one(r, total):
        pre = hid_ref[span(r, width), :].astype(F32) + row_ref[pl.ds(r, 1), :] + col_ref[...]
        sig = 0.5 * jnp.tanh(0.5 * pre) + 0.5
        ok = mask[...] > limit(r)
        act_ref[span(r, width), :] = jnp.where(ok, pre * sig, 0.0).astype(BF)
        here, after = span(r, width), span(r + 1, width)
        adj = jnp.where(low, adj_low[here, :].astype(F32), adj_high[here, :].astype(F32))
        grad = jnp.where(low, grad_low[after, :].astype(F32), grad_high[after, :].astype(F32))
        dz = adj * (sig * (1.0 + pre * (1.0 - sig)))
        next_ref[here, :] = (grad + dz).astype(BF)
        own = dz[edge : edge + breadth]
        inner = (r >= 1) & (r <= height)

        @pl.when(inner)
        def _():
            sums_ref[pl.ds(r - 1, 1), :] = jnp.sum(own, 0, keepdims=True)

        return total + jnp.where(inner, own, 0.0)

    sums_ref[pl.ds(height, breadth), :] = loop(height + 2, one, jnp.zeros((breadth, sums_ref.shape[1]), F32))
    send_sums(sums_ref, copies_ref)


def backward_kernel(
    dims, extent, part_ref, slope_ref, row_ref, col_ref, kernel_ref,
    grad_ref, next_ref, copies_ref, bias_ref, prod, sums_ref, mask,
):
    height, breadth, width = dims
    mask[...], limit = inside_limits(1, extent, height, breadth, width)
    edge = (width - breadth) // 2

    def full(r):
        return part_ref[span(r, width), :].astype(F32) + row_ref[pl.ds(r, 1), :] + col_ref[...]

    def round_row(r, carry):
        ok = mask[...] > limit(r)
        grad_ref[span(r, width), :] = jnp.where(ok, full(r), 0.0).astype(BF)
        return carry

    loop(height + 2, round_row, 0)
    zero = jnp.zeros((breadth, sums_ref.shape[1]), F32)

    def finish(r, value, carry):
        total, bias = carry
        dz = value * slope_ref[span(r + 2, width), :].astype(F32)
        own = dz[edge : edge + breadth]
        grad = full(r + 1)[edge : edge + breadth]
        sums_ref[pl.ds(r, 1), :] = jnp.sum(own, 0, keepdims=True)
        next_ref[pl.ds(pl.multiple_of(r * breadth, 16), breadth), :] = (grad + own).astype(BF)
        return total + own, bias + grad

    total, bias = convolve_rows(
        grad_ref, 0, kernel_ref, prod, height, width, 2, finish, (zero, zero), True
    )
    sums_ref[pl.ds(height, breadth), :] = total
    send_sums(sums_ref, copies_ref)
    bias_ref[...] = jnp.sum(bias, 0, keepdims=True)


def taps_kernel(dims, part_ref, row_ref, col_ref, tap_ref, bias_ref, full):
    height, breadth, up, channels = dims

    def one(r, total):
        at = pl.ds(pl.multiple_of(r * breadth, 16), breadth)
        value = part_ref[at, :].astype(F32) + row_ref[pl.ds(r, 1), :] + col_ref[...]
        full[at, :] = value
        return total + value

    total = loop(height, one, jnp.zeros(col_ref.shape, F32))
    bias_ref[...] = jnp.sum(total, 0, keepdims=True)
    tok_cols = breadth // up
    for i in range(height // up):
        for a in range(up):
            for b in range(up):
                piece = full[pl.ds((up * i + a) * breadth + b, tok_cols, stride=up), :]
                tap = a * up + b
                tap_ref[
                    i * tok_cols : (i + 1) * tok_cols, tap * channels : (tap + 1) * channels
                ] = piece.astype(BF)


def kernel_grad_kernel(dims, act_base, grad_base, act_ref, grad_ref, rounded_ref, wide, moved, out_ref):
    height, breadth, width = dims
    edge = (width - breadth) // 2
    channels = act_ref.shape[1]
    column = lax.broadcasted_iota(jnp.int32, (width, channels), 0)
    ok = (column >= edge) & (column < edge + breadth)
    wide[pl.ds(0, 8), :] = jnp.zeros((8, channels), F32)
    wide[pl.ds(8 + height * width, 8), :] = jnp.zeros((8, channels), F32)

    def fill(r, carry):
        if grad_base is None:
            value = grad_ref[span(r, breadth), :].astype(F32)
            rim = jnp.zeros((edge, channels), F32)
            value = jnp.concatenate([rim, value, rim], 0)
        else:
            value = jnp.where(ok, grad_ref[span(r + grad_base, width), :].astype(F32), 0.0)
        wide[span8(r * width + 8, width), :] = value
        return carry

    loop(height, fill, 0)

    def move(r, carry):
        view = wide.at[span8(r * width, width + 16), :]
        for dx in range(3):
            moved[span(r, width), dx * channels : (dx + 1) * channels] = view[
                9 - dx : 9 - dx + width, :
            ].astype(BF)
        return carry

    loop(height, move, 0)

    @pl.when(pl.program_id(0) == 0)
    def _():
        out_ref[...] = jnp.zeros(out_ref.shape, F32)

    chunks = 2
    step = height // chunks

    def chunk(index, carry):
        start = index * step
        lhs = jnp.concatenate(
            [act_ref[span(start + act_base + dy, width, step), :] for dy in range(3)], 1
        )
        result = lax.dot_general(
            lhs,
            moved[span(start, width, step), :],
            (((0,), (0,)), ((), ())),
            preferred_element_type=F32,
        )
        for tap in range(9):
            dy, dx = divmod(tap, 3)
            out_ref[tap * channels : (tap + 1) * channels, :] += result[
                dy * channels : (dy + 1) * channels, dx * channels : (dx + 1) * channels
            ]
        return carry

    lax.fori_loop(0, chunks, chunk, 0)

    @pl.when(pl.program_id(0) == pl.num_programs(0) - 1)
    def _():
        rounded_ref[...] = out_ref[...].astype(BF)


def plain_pass(tokens, gout, deconv_weight, deconv_bias, conv_kernels, conv_biases):
    objects, _, tok_rows, tok_cols, fan = tokens.shape
    _, _, height, breadth, channels = gout.shape
    planes = 3 * objects
    up = height // tok_rows
    extent = height * lax.axis_size("plane")
    row_start = lax.axis_index("plane") * height
    col_start = lax.axis_index("tile") * breadth
    place = (extent, row_start, col_start, height, breadth)
    ctx_place = (row_start, col_start, height, breadth)

    tok = tokens.reshape(planes, tok_rows, tok_cols, fan)
    grad_top = gout.reshape(planes, height, breadth, channels)
    tok_wide, grad_wide = grow_dim(tok, grad_top, "plane", 1, 1, 2)
    tok_wide, grad_wide = grow_dim(tok_wide, grad_wide, "tile", 2, 1, 2)

    taps = conv_kernels.reshape(2, 3, 3, channels, channels)
    back = taps[:, ::-1, ::-1].transpose(0, 1, 2, 4, 3)

    raw = jnp.dot(tok_wide.reshape(-1, fan), deconv_weight, preferred_element_type=F32)
    raw = raw.reshape(planes, tok_rows + 2, tok_cols + 2, up, up, channels)
    raw = raw.transpose(0, 1, 3, 2, 4, 5)
    raw = raw.reshape(planes, up * (tok_rows + 2), up * (tok_cols + 2), channels)
    raw = trim(raw, up - 2)

    own = trim(raw, 2)
    row0, col0 = band_sums(jnp.sum(own, 2), jnp.sum(own, 1))
    bias = deconv_bias
    pre0 = raw + bias + spread(
        row0 + extent * bias, col0 + extent * bias, extent, 2, *ctx_place
    )
    act0 = jnp.where(inside(2, *place), jax.nn.silu(pre0), 0.0).astype(BF)
    step0 = conv(act0, taps[0])

    own = trim(step0, 1)
    row1, col1 = band_sums(jnp.sum(own, 2), jnp.sum(own, 1))
    bias = deconv_bias + conv_biases[0]
    pre1 = trim(raw, 1) + step0 + bias + spread(
        row0 + row1 + extent * bias, col0 + col1 + extent * bias, extent, 1, *ctx_place
    )
    ok1 = inside(1, *place)
    act1 = jnp.where(ok1, jax.nn.silu(pre1), 0.0).astype(BF)

    dz1 = conv(grad_wide, back[1]) * slope(pre1)
    own = trim(dz1, 1)
    drow1, dcol1 = band_sums(jnp.sum(own, 2), jnp.sum(own, 1))
    kernel1 = kernel_gradient(act1, grad_top)
    cbias1 = jnp.sum(grad_top.astype(F32), (0, 1, 2))
    grad1 = trim(grad_wide, 1).astype(F32) + dz1 + spread(drow1, dcol1, extent, 1, *ctx_place)
    gb1 = jnp.where(ok1, grad1, 0.0).astype(BF)
    own1 = trim(grad1, 1)
    cbias0 = jnp.sum(own1, (0, 1, 2))

    dz0 = conv(gb1, back[0]) * slope(trim(pre0, 2))
    drow0, dcol0 = band_sums(jnp.sum(dz0, 2), jnp.sum(dz0, 1))
    kernel0 = kernel_gradient(trim(act0, 1), trim(gb1, 1))
    grad0 = own1 + dz0 + spread(drow0, dcol0, extent, 0, *ctx_place)
    bias_part = jnp.sum(grad0, (0, 1, 2))

    gb0 = grad0.astype(BF).reshape(planes, tok_rows, up, tok_cols, up, channels)
    tap_grads = gb0.transpose(0, 1, 3, 2, 4, 5).reshape(-1, up * up * channels)
    tok_grad = lax.dot_general(
        tap_grads, deconv_weight, (((1,), (1,)), ((), ())), preferred_element_type=F32
    )
    tok_grad = tok_grad.astype(BF).reshape(tokens.shape)
    weight_part = lax.dot_general(
        tok.reshape(-1, fan), tap_grads, (((0,), (0,)), ((), ())), preferred_element_type=F32
    )
    small = jnp.concatenate(
        [kernel0.reshape(-1, channels), kernel1.reshape(-1, channels)]
        + [v.reshape(1, channels) for v in (cbias0, cbias1)],
        0,
    )
    small = small_whole(small_summed(small_parts(small), bias_part))
    bands = lax.axis_size("plane") * lax.axis_size("tile")
    total = lax.axis_size("obj") * bands
    weight_grad = scatter_all(
        weight_part.reshape(total, fan // total, -1), (lax.axis_size("obj"), bands)
    )
    return (tok_grad, weight_grad) + small_results(small, conv_kernels.shape[1])


def sent_to_all(array, axes):
    copies = jnp.broadcast_to(array[None], (lax.axis_size(axes),) + array.shape)
    return lax.all_to_all(copies, axes, 0, 0, tiled=True)


def small_parts(small):
    rows, channels = small.shape
    bands = lax.axis_size(BANDS)
    piece = -(-rows // bands)
    piece += -piece % 16
    parts = jnp.pad(small, ((0, piece * bands - rows), (0, 0))).astype(BF)
    return lax.all_to_all(parts.reshape(bands, piece, channels), BANDS, 0, 0, tiled=True)


def small_summed(parts, bias_part):
    piece = jnp.sum(parts.astype(F32), 0)
    tail = jnp.pad(bias_part[None], ((0, 15), (0, 0)))
    return sent_to_all(jnp.concatenate([piece, tail], 0).astype(BF), "obj")


def small_whole(parts):
    return sent_to_all(jnp.sum(parts.astype(F32), 0).astype(BF), BANDS)


def small_results(parts, per_kernel):
    channels = parts.shape[-1]
    small = parts[:, :-16].reshape(-1, channels).astype(F32)
    bias = jnp.sum(parts[:, -16].astype(F32), 0)
    kernel_grads = small[: 2 * per_kernel].reshape(2, per_kernel, channels)
    return (bias, kernel_grads, small[2 * per_kernel : 2 * per_kernel + 2])


def bits_of(size):
    steps = []
    while size > 1:
        size //= 2
        steps.append(size)
    return steps


def halved(parts, dim, axis, step):
    upper = ((lax.axis_index(axis) // step) % 2).astype(jnp.int32)
    size = lax.axis_size(axis)
    mine = lax.dynamic_slice_in_dim(parts, upper, 1, dim)
    theirs = lax.dynamic_slice_in_dim(parts, 1 - upper, 1, dim)
    other = lax.ppermute(theirs, axis, [(i, i ^ step) for i in range(size)])
    return (mine.astype(F32) + other.astype(F32)).astype(BF)


def near_step():
    return ("plane", 1), 1 + len(bits_of(lax.axis_size("plane"))) - 1


def weight_parts(product):
    fan, columns = product.shape
    objs = lax.axis_size("obj")
    bits = len(bits_of(lax.axis_size("plane"))) + len(bits_of(lax.axis_size("tile")))
    shape = (objs,) + (2,) * bits + (fan // (objs * 2**bits), columns)
    step, dim = near_step()
    return halved(product.astype(BF).reshape(shape), dim, *step)


def weight_scattered(parts):
    objs = parts.shape[0]
    steps = [("plane", s) for s in bits_of(lax.axis_size("plane"))]
    steps += [("tile", s) for s in bits_of(lax.axis_size("tile"))]
    rest = [(i + 1, step) for i, step in enumerate(steps) if i + 1 != near_step()[1]]
    streams = [parts[: objs // 2], parts[objs // 2 :]]
    for one, two in zip(rest, reversed(rest)):
        streams[0] = halved(streams[0], one[0], *one[1])
        streams[1] = halved(streams[1], two[0], *two[1])
    return jnp.concatenate(streams, 0).reshape(objs, *parts.shape[-2:])


def kernel_pass(tokens, gout, deconv_weight, deconv_bias, conv_kernels, conv_biases):
    objects, _, tok_rows, tok_cols, fan = tokens.shape
    _, _, height, breadth, channels = gout.shape
    planes = 3 * objects
    up = height // tok_rows
    edge = 8
    width = breadth + 2 * edge
    extent = height * lax.axis_size("plane")
    row_start = lax.axis_index("plane") * height
    col_start = lax.axis_index("tile") * breadth
    dims = (height, breadth, width)

    tok = tokens.reshape(planes, tok_rows, tok_cols, fan)
    grad_top = gout.reshape(planes, height, breadth, channels)
    flat_tok = lambda array: array.reshape(planes, -1, fan)
    flat_grad = lambda array: array.reshape(planes, -1, channels)

    def columns_beside(bands_of, last):
        def cut(parts):
            cells = [p[:, :, -2:] if last else p[:, :, :2] for p in parts]
            return jnp.concatenate([c.astype(BF) for c in cells], 1)

        rim = shifted(jnp.stack([cut(parts) for parts in bands_of], 2), "tile", 1 if last else -1)
        room = (edge - 2, 0) if last else (0, edge - 2)
        return flat_grad(jnp.pad(rim, ((0, 0),) * 3 + (room, (0, 0))).astype(F32))

    taps = conv_kernels.reshape(2, 3, 3, channels, channels)
    side = 3 * channels
    ahead = taps[0].transpose(0, 2, 1, 3).reshape(side, side)
    back = taps.transpose(0, 1, 4, 2, 3).reshape(2, side, side)

    flat = lambda rows: (planes, rows * width, channels)
    bands = lax.axis_size(BANDS)
    copies = ((bands, planes, height + breadth, channels), BF, "copies")
    sums = pltpu.VMEM((height + breadth, channels), F32)
    one = ((planes, 1, channels), F32, False)
    prod = lambda rows: pltpu.VMEM((rows * width + 16, side), F32)
    conv_flops = lambda rows: 2 * rows * width * side * side
    mask = pltpu.VMEM((width, channels), F32)

    def contexts(parts, rim, pad, bias, beside=None):
        parts = lax.all_to_all(parts, BANDS, 0, 0, tiled=True)
        if beside is not None:
            parts, beside = lax.optimization_barrier((parts, beside))
        whole = lambda array: pl.BlockSpec(memory_space=pltpu.VMEM)
        shapes = [
            jax.ShapeDtypeStruct((planes, height + 2 * rim, channels), F32),
            jax.ShapeDtypeStruct((planes, breadth + 2 * pad, channels), F32),
        ]
        terms = pl.pallas_call(
            functools.partial(context_kernel, dims, rim, pad),
            in_specs=[whole(parts), whole(bias)],
            out_specs=[whole(shape) for shape in shapes],
            out_shape=shapes,
            scratch_shapes=[pltpu.VMEM((3, extent + 16, channels), F32)] * 2,
            compiler_params=pltpu.CompilerParams(vmem_limit_bytes=60 << 20),
            cost_estimate=pl.CostEstimate(
                flops=4 * parts.size, bytes_accessed=2 * parts.size, transcendentals=0
            ),
        )(parts, bias.reshape(1, channels))
        return tuple(terms) if beside is None else tuple(terms) + (beside,)

    rim_rows = ((planes, 4 * breadth, channels), BF, False)
    raw, parts, first, last, cbias1 = call(
        functools.partial(upsample_kernel, (tok_rows, tok_cols, up, height, breadth, channels)),
        planes,
        [(flat_tok(tok), False), (flat_grad(grad_top), False), (deconv_weight, True)],
        [((planes, height * breadth, channels), F32, False), copies, rim_rows, rim_rows, one],
        [sums],
        flops=2 * tok_rows * tok_cols * fan * up * up * channels,
    )
    half = planes // 2
    above, below = shifted(last, "plane", 1), shifted(first, "plane", -1)
    slots = lambda array: array.reshape(planes, 2, 2, breadth, channels)
    beyond = (slots(above), slots(below))
    both = [
        (beyond[0][:, slot], cells, beyond[1][:, slot])
        for slot, cells in enumerate((grad_top, raw.reshape(grad_top.shape)))
    ]
    left, right = columns_beside(both, True), columns_beside(both, False)

    def adjoint_of(first, count):
        kind = (first, -count)
        return call(
            functools.partial(adjoint_kernel, dims),
            count,
            [(flat_grad(grad_top), kind)]
            + [(array, kind) for array in (above, below, left, right)]
            + [(back[1], True)],
            [
                ((count, (height + 4) * width, channels), BF, False),
                ((count, (height + 2) * width, channels), BF, False),
            ],
            [prod(height // 2 + 1)],
            conv_flops(height + 2),
        )

    low = adjoint_of(0, half)
    row_ctx, col_ctx, low = contexts(parts, 2, edge, deconv_bias, low)
    act0, slope0, hidden, parts = call(
        functools.partial(forward_kernel, dims, extent),
        planes,
        [(raw, False)]
        + [(array, False) for array in (above, below, left, right)]
        + [(row_ctx, False), (col_ctx, False)]
        + [(ahead, True)],
        [(flat(height + 4), BF, False)] * 2 + [(flat(height + 2), BF, False), copies],
        [pltpu.VMEM(flat(height + 4)[1:], F32), prod(height // 2 + 1), sums, mask],
        conv_flops(height + 2),
    )
    high = adjoint_of(half, planes - half)
    row_ctx, col_ctx, high = contexts(parts, 1, edge, deconv_bias + conv_biases[0], high)
    act1, part1, parts = call(
        functools.partial(middle_kernel, dims, extent, half),
        planes,
        [(hidden, False)]
        + [(low[1], (0, half)), (high[1], (half, planes - half))]
        + [(low[0], (0, half)), (high[0], (half, planes - half))]
        + [(row_ctx, False), (col_ctx, False)],
        [(flat(height + 2), BF, False), (flat(height + 2), BF, False), copies],
        [sums, mask],
    )

    def kernel_gradient_of(act, grad, act_base, grad_base):
        (result,) = call(
            functools.partial(kernel_grad_kernel, dims, act_base, grad_base),
            planes,
            [(act, False), (grad, False)],
            [((9 * channels, channels), BF, True)],
            [
                pltpu.VMEM((height * width + 16, channels), F32),
                pltpu.VMEM((height * width, side), BF),
                pltpu.VMEM((9 * channels, channels), F32),
            ],
            2 * height * width * side * side,
        )
        return result

    none = jnp.zeros((channels,), F32)
    kernel1 = kernel_gradient_of(act1, flat_grad(grad_top), 0, None)
    row_ctx, col_ctx, kernel1 = contexts(parts, 1, edge, none, kernel1)
    gb1, part0, parts, cbias0 = call(
        functools.partial(backward_kernel, dims, extent),
        planes,
        [(part1, False), (slope0, False), (row_ctx, False), (col_ctx, False)]
        + [(back[0], True)],
        [(flat(height + 2), BF, False), ((planes, height * breadth, channels), BF, False)]
        + [copies, one],
        [prod(height // 2), sums, mask],
        conv_flops(height),
    )
    kernel0 = kernel_gradient_of(act0, gb1, 1, 1)
    row_ctx, col_ctx, kernel0 = contexts(parts, 0, 0, none, kernel0)
    small = small_parts(
        jnp.concatenate(
            [kernel0, kernel1] + [jnp.sum(v, 0).astype(BF) for v in (cbias0, cbias1)], 0
        )
    )
    tap_grads, bias_part = call(
        functools.partial(taps_kernel, (height, breadth, up, channels)),
        planes,
        [(part0, False), (row_ctx, False), (col_ctx, False)],
        [((planes, tok_rows * tok_cols, up * up * channels), BF, False), one],
        [pltpu.VMEM((height * breadth, channels), F32)],
    )
    tap_grads = tap_grads.reshape(-1, up * up * channels)
    tap_grads, small = lax.optimization_barrier((tap_grads, small))
    product = lax.dot_general(
        tok.reshape(-1, fan), tap_grads, (((0,), (0,)), ((), ())), preferred_element_type=F32
    )
    small = small_summed(small, jnp.sum(bias_part, (0, 1)))
    parts = weight_parts(product)
    tok_grad = lax.dot_general(
        tap_grads, deconv_weight, (((1,), (1,)), ((), ())), preferred_element_type=F32
    )
    tok_grad = tok_grad.astype(BF).reshape(tokens.shape)
    parts, small, tok_grad = lax.optimization_barrier((parts, small, tok_grad))
    small = small_whole(small)
    parts, small = lax.optimization_barrier((weight_scattered(parts), small))
    weight_grad = scattered(parts, "obj")
    return (tok_grad, weight_grad) + small_results(small, conv_kernels.shape[1])


def per_device(tokens, gout, deconv_weight, deconv_bias, conv_kernels, conv_biases):
    channels = gout.shape[-1]
    sizes = [lax.axis_size(axis) for axis in ("obj", "plane", "tile")]
    fits = gout.shape[3] % 16 == 0 and gout.shape[2] % 16 == 0 and channels % 128 == 0
    fits = fits and all(size & (size - 1) == 0 and size > 1 for size in sizes)
    run = kernel_pass if fits else plain_pass
    return run(tokens, gout, deconv_weight, deconv_bias, conv_kernels, conv_biases)


def solution(mesh):
    placed = (
        P("obj", None, "plane", "tile", None),
        P("obj", None, "plane", "tile", None),
        P(),
        P(),
        P(),
        P(),
    )
    return jax.shard_map(
        per_device,
        mesh=mesh,
        in_specs=placed,
        out_specs=(
            P("obj", None, "plane", "tile", None),
            P(EVERY, None),
            P(),
            P(),
            P(),
        ),
        check_vma=False,
    )
```

```python
import functools

import jax
import jax.numpy as jnp
from jax import lax
from jax.experimental import pallas as pl
from jax.experimental.pallas import tpu as pltpu
from jax.sharding import PartitionSpec as P

BANDS = ("plane", "tile")
EVERY = ("obj", "plane", "tile")
CONV_DIMS = ("NHWC", "HWIO", "NHWC")
BF = jnp.bfloat16
F32 = jnp.float32


def shifted(array, axis, step):
    size = lax.axis_size(axis)
    pairs = [(i, i + step) for i in range(size) if 0 <= i + step < size]
    return lax.ppermute(array, axis, pairs)


def grow_dim(tok, grad, axis, dim, tok_rim, grad_rim):
    planes, lanes = tok.shape[0], grad.shape[-1]

    def cut(array, rim, last):
        length = array.shape[dim]
        start = length - rim if last else 0
        return lax.slice_in_dim(array, start, start + rim, axis=dim)

    def pack(last):
        parts = [cut(tok, tok_rim, last), cut(grad, grad_rim, last)]
        return jnp.concatenate([part.reshape(planes, -1, lanes) for part in parts], 1)

    def unpack(packed):
        shapes = [cut(tok, tok_rim, False).shape, cut(grad, grad_rim, False).shape]
        rows = shapes[0][1] * shapes[0][2] * shapes[0][3] // lanes
        return packed[:, :rows].reshape(shapes[0]), packed[:, rows:].reshape(shapes[1])

    before = unpack(shifted(pack(True), axis, 1))
    after = unpack(shifted(pack(False), axis, -1))
    return [
        jnp.concatenate([low, mid, high], axis=dim)
        for low, mid, high in zip(before, (tok, grad), after)
    ]


def band_sums(rows, cols):
    height = rows.shape[1]

    def joined(own, other, axis, step):
        upper = (lax.axis_index(axis) & step) != 0
        return jnp.where(
            upper, jnp.concatenate([other, own], 1), jnp.concatenate([own, other], 1)
        )

    rows, cols = rows.astype(BF), cols.astype(BF)
    for axis in ("tile", "plane"):
        size, step = lax.axis_size(axis), 1
        while step < size:
            height = rows.shape[1]
            other = lax.ppermute(
                jnp.concatenate([rows, cols], 1), axis, [(i, i ^ step) for i in range(size)]
            )
            other_rows, other_cols = other[:, :height], other[:, height:]
            if axis == "tile":
                rows = (rows.astype(F32) + other_rows.astype(F32)).astype(BF)
                cols = joined(cols, other_cols, axis, step)
            else:
                rows = joined(rows, other_rows, axis, step)
                cols = (cols.astype(F32) + other_cols.astype(F32)).astype(BF)
            step *= 2
    return rows.astype(F32), cols.astype(F32)


def spread(row_sum, col_sum, extent, ring, row_start, col_start, height, breadth):
    planes, _, channels = row_sum.shape
    rows = row_sum.reshape(planes // 3, 3, extent, channels) / extent
    cols = col_sum.reshape(planes // 3, 3, extent, channels) / extent
    row_ctx = jnp.stack([rows[:, 1], rows[:, 0], cols[:, 0]], 1)
    col_ctx = jnp.stack([rows[:, 2], cols[:, 2], cols[:, 1]], 1)

    def band(ctx, start, length):
        ctx = jnp.pad(ctx, ((0, 0), (0, 0), (ring, ring), (0, 0)))
        ctx = lax.dynamic_slice_in_dim(ctx, start, length + 2 * ring, 2)
        return ctx.reshape(planes, length + 2 * ring, channels)

    row_band = band(row_ctx, row_start, height)
    col_band = band(col_ctx, col_start, breadth)
    return row_band[:, :, None, :] + col_band[:, None, :, :]


def inside(ring, extent, row_start, col_start, height, breadth):
    row = row_start - ring + lax.iota(jnp.int32, height + 2 * ring)
    col = col_start - ring + lax.iota(jnp.int32, breadth + 2 * ring)
    row_ok = (row >= 0) & (row < extent)
    col_ok = (col >= 0) & (col < extent)
    return (row_ok[:, None] & col_ok[None, :])[None, :, :, None]


def conv(padded, kernel):
    return lax.conv_general_dilated(
        padded, kernel, (1, 1), "VALID", dimension_numbers=CONV_DIMS, preferred_element_type=F32
    )


def kernel_gradient(padded, grad):
    return lax.conv_general_dilated(
        padded,
        grad,
        (1, 1),
        "VALID",
        dimension_numbers=("CHWN", "IHWO", "HWNC"),
        preferred_element_type=F32,
    )


def trim(array, ring):
    return array[:, ring:-ring, ring:-ring, :]


def slope(pre):
    sig = jax.nn.sigmoid(pre)
    return sig * (1.0 + pre * (1.0 - sig))


def scattered(parts, axes):
    return jnp.sum(lax.all_to_all(parts, axes, 0, 0, tiled=True).astype(F32), 0)


def scatter_all(blocks, sizes):
    objs, bands = sizes
    blocks = blocks.astype(BF).reshape((objs, bands) + blocks.shape[1:])
    blocks = jnp.moveaxis(blocks, 1, 0)
    part = scattered(blocks, BANDS).astype(BF)
    return scattered(part, "obj")


def call(kernel, planes, ins, outs, scratch=(), flops=0):
    def spec(shape, kind):
        rest = (0,) * (len(shape) - 1)
        if kind is True:
            return pl.BlockSpec(shape, lambda p: (0,) + rest)
        if kind == "copies":
            return pl.BlockSpec(
                (shape[0], None) + shape[2:], lambda p: (0, p) + (0,) * (len(shape) - 2)
            )
        if kind is False:
            return pl.BlockSpec((None,) + shape[1:], lambda p: (p,) + rest)
        first, count = kind
        if count < 0:
            return pl.BlockSpec((None,) + shape[1:], lambda p: (p + first,) + rest)
        return pl.BlockSpec(
            (None,) + shape[1:], lambda p: (jnp.clip(p - first, 0, count - 1),) + rest
        )

    moved = sum(a.size * a.dtype.itemsize for a, _ in ins)
    return pl.pallas_call(
        kernel,
        grid=(planes,),
        in_specs=[spec(a.shape, kind) for a, kind in ins],
        out_specs=[spec(shape, kind) for shape, _, kind in outs],
        out_shape=[jax.ShapeDtypeStruct(shape, dtype) for shape, dtype, _ in outs],
        scratch_shapes=list(scratch),
        compiler_params=pltpu.CompilerParams(
            dimension_semantics=("arbitrary",), vmem_limit_bytes=60 << 20
        ),
        cost_estimate=pl.CostEstimate(
            flops=flops * planes, bytes_accessed=2 * moved, transcendentals=0
        ),
    )(*[a for a, _ in ins])


def inside_limits(ring, extent, height, breadth, width):
    row_start = lax.axis_index("plane") * height
    col_start = lax.axis_index("tile") * breadth
    edge = (width - breadth) // 2
    column = lax.broadcasted_iota(jnp.int32, (width, 128), 0) - edge
    ok = (column >= -ring) & (column < breadth + ring)
    ok = ok & (col_start + column >= 0) & (col_start + column < extent)
    ones = jnp.where(ok, 1.0, 0.0)

    def limit(r):
        row = row_start + r - ring
        return jnp.where((row >= 0) & (row < extent), 0.5, 2.0)

    return ones, limit


def span(row, width, rows=1):
    return pl.ds(pl.multiple_of(row * width, 16), rows * width)


def span8(start, size):
    return pl.ds(pl.multiple_of(start, 8), size)


def loop(rows, body, carry=None, unroll=4):
    return lax.fori_loop(0, rows, body, carry, unroll=unroll)


def convolve_rows(
    src, base, kernel_ref, prod, rows_out, width, chunks, finish, carry, flipped=False
):
    step = rows_out // chunks
    size = step * width
    order = (2, 1, 0) if flipped else (0, 1, 2)

    def chunk(index, carry):
        start = base + index * step
        lhs = jnp.concatenate([src[span(start + dy, width, step), :] for dy in order], 1)
        prod[pl.ds(8, size), :] = jnp.dot(lhs, kernel_ref[...], preferred_element_type=F32)
        channels = prod.shape[1] // 3

        def row(r, carry):
            view = prod.at[span8(r * width, width + 16), :]
            first, _, last = order
            value = (
                view[7 + first : 7 + first + width, :channels]
                + view[8 : 8 + width, channels : 2 * channels]
                + view[7 + last : 7 + last + width, 2 * channels :]
            )
            return finish(index * step + r, value, carry)

        return loop(step, row, carry)

    return lax.fori_loop(0, chunks, chunk, carry)


def send_sums(sums, copies_ref):
    for copy in range(copies_ref.shape[0]):
        copies_ref[copy] = sums[...].astype(BF)


def place_row(rows, r, slot, center, left_ref, right_ref):
    side = left_ref.shape[0] // rows // 2
    at = span8((2 * r + slot) * side, side)
    return jnp.concatenate([left_ref[at, :], center, right_ref[at, :]], 0)


def place_rows(rows, breadth, slot, refs, put):
    own_ref, above_ref, below_ref, left_ref, right_ref = refs

    def one(r, ref, at):
        center = ref[at, :].astype(F32)
        put(r, place_row(rows, r, slot, center, left_ref, right_ref))

    for r in range(2):
        at = (2 * slot + r) * breadth
        one(r, above_ref, slice(at, at + breadth))
        one(rows - 2 + r, below_ref, slice(at, at + breadth))

    def inner(r, carry):
        one(r + 2, own_ref, span(r, breadth))
        return carry

    loop(rows - 4, inner, 0)


def upsample_kernel(
    dims, tok_ref, grad_ref, weight_ref,
    raw_ref, copies_ref, first_ref, last_ref, bias_ref, sums,
):
    tok_rows, tok_cols, up, height, breadth, channels = dims
    cut = up * channels
    for a in range(up):
        weight = weight_ref[:, a * cut : (a + 1) * cut]
        prod = jnp.dot(tok_ref[...], weight, preferred_element_type=F32)
        for b in range(up):
            for i in range(tok_rows):
                raw_ref[pl.ds((up * i + a) * breadth + b, tok_cols, stride=up), :] = prod[
                    i * tok_cols : (i + 1) * tok_cols, b * channels : (b + 1) * channels
                ]

    def add(r, total):
        own = raw_ref[span(r, breadth), :]
        sums[pl.ds(r, 1), :] = jnp.sum(own, 0, keepdims=True)
        total, bias = total
        return total + own, bias + grad_ref[span(r, breadth), :].astype(F32)

    zero = jnp.zeros((breadth, channels), F32)
    total, bias = loop(height, add, (zero, zero))
    sums[pl.ds(height, breadth), :] = total
    bias_ref[...] = jnp.sum(bias, 0, keepdims=True)
    send_sums(sums, copies_ref)
    rim = 2 * breadth
    tail = slice((height - 2) * breadth, height * breadth)
    for ref, at in ((first_ref, slice(0, rim)), (last_ref, tail)):
        ref[:rim, :] = grad_ref[at, :]
        ref[rim:, :] = raw_ref[at, :].astype(BF)


def forward_kernel(
    dims, extent, row_ref, col_ref, own_ref, above_ref, below_ref, left_ref, right_ref, kernel_ref,
    act_ref, slope_ref, next_ref, copies_ref, raw_ref, prod, sums_ref, mask,
):
    height, breadth, width = dims
    mask[...], limit = inside_limits(2, extent, height, breadth, width)
    edge = (width - breadth) // 2

    def activate(r, value):
        raw_ref[span(r, width), :] = value
        pre = value + row_ref[pl.ds(r, 1), :] + col_ref[...]
        sig = 0.5 * jnp.tanh(0.5 * pre) + 0.5
        ok = mask[...] > limit(r)
        act_ref[span(r, width), :] = jnp.where(ok, pre * sig, 0.0).astype(BF)
        slope_ref[span(r, width), :] = (sig * (1.0 + pre * (1.0 - sig))).astype(BF)

    refs = (own_ref, above_ref, below_ref, left_ref, right_ref)
    place_rows(height + 4, breadth, 1, refs, activate)
    zero = jnp.zeros((breadth, sums_ref.shape[1]), F32)

    def finish(r, value, total):
        value = raw_ref[span(r + 1, width), :] + value
        next_ref[span(r, width), :] = value.astype(BF)
        own = value[edge : edge + breadth]
        inner = (r >= 1) & (r <= height)

        @pl.when(inner)
        def _():
            sums_ref[pl.ds(r - 1, 1), :] = jnp.sum(own, 0, keepdims=True)

        return total + jnp.where(inner, own, 0.0)

    sums_ref[pl.ds(height, breadth), :] = convolve_rows(
        act_ref, 0, kernel_ref, prod, height + 2, width, 2, finish, zero
    )
    send_sums(sums_ref, copies_ref)


def adjoint_kernel(
    dims, own_ref, above_ref, below_ref, left_ref, right_ref, kernel_ref, wide_ref, out_ref, prod
):
    height, breadth, width = dims

    def put(r, row):
        wide_ref[span(r, width), :] = row.astype(BF)

    refs = (own_ref, above_ref, below_ref, left_ref, right_ref)
    place_rows(height + 4, breadth, 0, refs, put)

    def finish(r, value, carry):
        out_ref[span(r, width), :] = value.astype(BF)
        return carry

    convolve_rows(wide_ref, 0, kernel_ref, prod, height + 2, width, 2, finish, 0, True)


def context_kernel(dims, ring, side, parts_ref, bias_ref, row_ref, col_ref, rows, cols):
    height, breadth, _ = dims
    bands, planes = parts_ref.shape[:2]
    extent = rows.shape[1] - 16
    down, across = extent // height, extent // breadth
    rows[...] = jnp.zeros(rows.shape, F32)
    cols[...] = jnp.zeros(cols.shape, F32)
    scale = 1.0 / extent
    for first in range(0, planes, 3):
        for q in range(3):
            part = lambda p, t, at, size: parts_ref[p * across + t, first + q, at : at + size, :].astype(F32)
            for p in range(down):
                pieces = [part(p, t, 0, height) for t in range(across)]
                rows[q, 8 + p * height : 8 + (p + 1) * height, :] = scale * sum(pieces)
            for t in range(across):
                pieces = [part(p, t, height, breadth) for p in range(down)]
                cols[q, 8 + t * breadth : 8 + (t + 1) * breadth, :] = scale * sum(pieces)
        row_at = span8(lax.axis_index("plane") * height, height + 16)
        col_at = span8(lax.axis_index("tile") * breadth, breadth + 16)
        for q, (ref, other) in enumerate(((rows, 1), (rows, 0), (cols, 0))):
            view = ref.at[other, row_at, :]
            row_ref[first + q] = view[8 - ring : 8 + height + ring, :] + 2.0 * bias_ref[...]
        for q, (ref, other) in enumerate(((rows, 2), (cols, 2), (cols, 1))):
            view = ref.at[other, col_at, :]
            col_ref[first + q] = view[8 - side : 8 + breadth + side, :] + bias_ref[...]


def with_contexts(kernel, dims, ring, side):
    def body(parts_ref, bias_ref, *refs):
        row_all, col_all, rows, cols = refs[-4:]

        @pl.when(pl.program_id(0) == 0)
        def _():
            context_kernel(
                dims, ring, side, parts_ref, bias_ref, row_all, col_all, rows, cols
            )

        plane = pl.program_id(0)
        kernel(row_all.at[plane], col_all.at[plane], *refs[:-4])

    return body


def middle_kernel(
    dims, extent, half, row_ref, col_ref, hid_ref, adj_low, adj_high, grad_low, grad_high, act_ref, next_ref, copies_ref, sums_ref, mask,
):
    height, breadth, width = dims
    mask[...], limit = inside_limits(1, extent, height, breadth, width)
    low = pl.program_id(0) < half
    edge = (width - breadth) // 2

    def one(r, total):
        pre = hid_ref[span(r, width), :].astype(F32) + row_ref[pl.ds(r, 1), :] + col_ref[...]
        sig = 0.5 * jnp.tanh(0.5 * pre) + 0.5
        ok = mask[...] > limit(r)
        act_ref[span(r, width), :] = jnp.where(ok, pre * sig, 0.0).astype(BF)
        here, after = span(r, width), span(r + 1, width)
        adj = jnp.where(low, adj_low[here, :].astype(F32), adj_high[here, :].astype(F32))
        grad = jnp.where(low, grad_low[after, :].astype(F32), grad_high[after, :].astype(F32))
        dz = adj * (sig * (1.0 + pre * (1.0 - sig)))
        next_ref[here, :] = (grad + dz).astype(BF)
        own = dz[edge : edge + breadth]
        inner = (r >= 1) & (r <= height)

        @pl.when(inner)
        def _():
            sums_ref[pl.ds(r - 1, 1), :] = jnp.sum(own, 0, keepdims=True)

        return total + jnp.where(inner, own, 0.0)

    sums_ref[pl.ds(height, breadth), :] = loop(height + 2, one, jnp.zeros((breadth, sums_ref.shape[1]), F32))
    send_sums(sums_ref, copies_ref)


def backward_kernel(
    dims, extent, row_ref, col_ref, part_ref, slope_ref, kernel_ref,
    grad_ref, next_ref, copies_ref, bias_ref, prod, sums_ref, mask,
):
    height, breadth, width = dims
    mask[...], limit = inside_limits(1, extent, height, breadth, width)
    edge = (width - breadth) // 2

    def full(r):
        return part_ref[span(r, width), :].astype(F32) + row_ref[pl.ds(r, 1), :] + col_ref[...]

    def round_row(r, carry):
        ok = mask[...] > limit(r)
        grad_ref[span(r, width), :] = jnp.where(ok, full(r), 0.0).astype(BF)
        return carry

    loop(height + 2, round_row, 0)
    zero = jnp.zeros((breadth, sums_ref.shape[1]), F32)

    def finish(r, value, carry):
        total, bias = carry
        dz = value * slope_ref[span(r + 2, width), :].astype(F32)
        own = dz[edge : edge + breadth]
        grad = full(r + 1)[edge : edge + breadth]
        sums_ref[pl.ds(r, 1), :] = jnp.sum(own, 0, keepdims=True)
        next_ref[pl.ds(pl.multiple_of(r * breadth, 16), breadth), :] = (grad + own).astype(BF)
        return total + own, bias + grad

    total, bias = convolve_rows(
        grad_ref, 0, kernel_ref, prod, height, width, 2, finish, (zero, zero), True
    )
    sums_ref[pl.ds(height, breadth), :] = total
    send_sums(sums_ref, copies_ref)
    bias_ref[...] = jnp.sum(bias, 0, keepdims=True)


def taps_kernel(dims, row_ref, col_ref, part_ref, tap_ref, bias_ref, full):
    height, breadth, up, channels = dims

    def one(r, total):
        at = pl.ds(pl.multiple_of(r * breadth, 16), breadth)
        value = part_ref[at, :].astype(F32) + row_ref[pl.ds(r, 1), :] + col_ref[...]
        full[at, :] = value
        return total + value

    total = loop(height, one, jnp.zeros(col_ref.shape, F32))
    bias_ref[...] = jnp.sum(total, 0, keepdims=True)
    tok_cols = breadth // up
    for i in range(height // up):
        for a in range(up):
            for b in range(up):
                piece = full[pl.ds((up * i + a) * breadth + b, tok_cols, stride=up), :]
                tap = a * up + b
                tap_ref[
                    i * tok_cols : (i + 1) * tok_cols, tap * channels : (tap + 1) * channels
                ] = piece.astype(BF)


def kernel_grad_kernel(dims, act_base, grad_base, act_ref, grad_ref, *refs):
    more, (rounded_ref, wide, moved, out_ref) = refs[:-4], refs[-4:]

    height, breadth, width = dims
    edge = (width - breadth) // 2
    channels = act_ref.shape[1]
    column = lax.broadcasted_iota(jnp.int32, (width, channels), 0)
    ok = (column >= edge) & (column < edge + breadth)
    wide[pl.ds(0, 8), :] = jnp.zeros((8, channels), F32)
    wide[pl.ds(8 + height * width, 8), :] = jnp.zeros((8, channels), F32)

    def fill(r, carry):
        if grad_base is None:
            value = grad_ref[span(r, breadth), :].astype(F32)
            rim = jnp.zeros((edge, channels), F32)
            value = jnp.concatenate([rim, value, rim], 0)
        else:
            value = jnp.where(ok, grad_ref[span(r + grad_base, width), :].astype(F32), 0.0)
        wide[span8(r * width + 8, width), :] = value
        return carry

    loop(height, fill, 0)

    def move(r, carry):
        view = wide.at[span8(r * width, width + 16), :]
        for dx in range(3):
            moved[span(r, width), dx * channels : (dx + 1) * channels] = view[
                9 - dx : 9 - dx + width, :
            ].astype(BF)
        return carry

    loop(height, move, 0)

    @pl.when(pl.program_id(0) == 0)
    def _():
        out_ref[...] = jnp.zeros(out_ref.shape, F32)

    chunks = 2
    step = height // chunks

    def chunk(index, carry):
        start = index * step
        lhs = jnp.concatenate(
            [act_ref[span(start + act_base + dy, width, step), :] for dy in range(3)], 1
        )
        result = lax.dot_general(
            lhs,
            moved[span(start, width, step), :],
            (((0,), (0,)), ((), ())),
            preferred_element_type=F32,
        )
        for tap in range(9):
            dy, dx = divmod(tap, 3)
            out_ref[tap * channels : (tap + 1) * channels, :] += result[
                dy * channels : (dy + 1) * channels, dx * channels : (dx + 1) * channels
            ]
        return carry

    lax.fori_loop(0, chunks, chunk, 0)

    @pl.when(pl.program_id(0) == pl.num_programs(0) - 1)
    def _():
        size = out_ref.shape[0]
        rounded_ref[:size, :] = out_ref[...].astype(BF)
        if more:
            other_ref, bias0_ref, bias1_ref = more
            rounded_ref[size : 2 * size, :] = other_ref[...]
            tail = rounded_ref.shape[0] - 2 * size
            row = lax.broadcasted_iota(jnp.int32, (tail, channels), 0)
            bias0 = jnp.sum(bias0_ref[...], 0)
            bias1 = jnp.sum(bias1_ref[...], 0)
            value = jnp.where(row == 0, bias0, jnp.where(row == 1, bias1, 0.0))
            rounded_ref[2 * size :, :] = value.astype(BF)


def plain_pass(tokens, gout, deconv_weight, deconv_bias, conv_kernels, conv_biases):
    objects, _, tok_rows, tok_cols, fan = tokens.shape
    _, _, height, breadth, channels = gout.shape
    planes = 3 * objects
    up = height // tok_rows
    extent = height * lax.axis_size("plane")
    row_start = lax.axis_index("plane") * height
    col_start = lax.axis_index("tile") * breadth
    place = (extent, row_start, col_start, height, breadth)
    ctx_place = (row_start, col_start, height, breadth)

    tok = tokens.reshape(planes, tok_rows, tok_cols, fan)
    grad_top = gout.reshape(planes, height, breadth, channels)
    tok_wide, grad_wide = grow_dim(tok, grad_top, "plane", 1, 1, 2)
    tok_wide, grad_wide = grow_dim(tok_wide, grad_wide, "tile", 2, 1, 2)

    taps = conv_kernels.reshape(2, 3, 3, channels, channels)
    back = taps[:, ::-1, ::-1].transpose(0, 1, 2, 4, 3)

    raw = jnp.dot(tok_wide.reshape(-1, fan), deconv_weight, preferred_element_type=F32)
    raw = raw.reshape(planes, tok_rows + 2, tok_cols + 2, up, up, channels)
    raw = raw.transpose(0, 1, 3, 2, 4, 5)
    raw = raw.reshape(planes, up * (tok_rows + 2), up * (tok_cols + 2), channels)
    raw = trim(raw, up - 2)

    own = trim(raw, 2)
    row0, col0 = band_sums(jnp.sum(own, 2), jnp.sum(own, 1))
    bias = deconv_bias
    pre0 = raw + bias + spread(
        row0 + extent * bias, col0 + extent * bias, extent, 2, *ctx_place
    )
    act0 = jnp.where(inside(2, *place), jax.nn.silu(pre0), 0.0).astype(BF)
    step0 = conv(act0, taps[0])

    own = trim(step0, 1)
    row1, col1 = band_sums(jnp.sum(own, 2), jnp.sum(own, 1))
    bias = deconv_bias + conv_biases[0]
    pre1 = trim(raw, 1) + step0 + bias + spread(
        row0 + row1 + extent * bias, col0 + col1 + extent * bias, extent, 1, *ctx_place
    )
    ok1 = inside(1, *place)
    act1 = jnp.where(ok1, jax.nn.silu(pre1), 0.0).astype(BF)

    dz1 = conv(grad_wide, back[1]) * slope(pre1)
    own = trim(dz1, 1)
    drow1, dcol1 = band_sums(jnp.sum(own, 2), jnp.sum(own, 1))
    kernel1 = kernel_gradient(act1, grad_top)
    cbias1 = jnp.sum(grad_top.astype(F32), (0, 1, 2))
    grad1 = trim(grad_wide, 1).astype(F32) + dz1 + spread(drow1, dcol1, extent, 1, *ctx_place)
    gb1 = jnp.where(ok1, grad1, 0.0).astype(BF)
    own1 = trim(grad1, 1)
    cbias0 = jnp.sum(own1, (0, 1, 2))

    dz0 = conv(gb1, back[0]) * slope(trim(pre0, 2))
    drow0, dcol0 = band_sums(jnp.sum(dz0, 2), jnp.sum(dz0, 1))
    kernel0 = kernel_gradient(trim(act0, 1), trim(gb1, 1))
    grad0 = own1 + dz0 + spread(drow0, dcol0, extent, 0, *ctx_place)
    bias_part = jnp.sum(grad0, (0, 1, 2))

    gb0 = grad0.astype(BF).reshape(planes, tok_rows, up, tok_cols, up, channels)
    tap_grads = gb0.transpose(0, 1, 3, 2, 4, 5).reshape(-1, up * up * channels)
    tok_grad = lax.dot_general(
        tap_grads, deconv_weight, (((1,), (1,)), ((), ())), preferred_element_type=F32
    )
    tok_grad = tok_grad.astype(BF).reshape(tokens.shape)
    weight_part = lax.dot_general(
        tok.reshape(-1, fan), tap_grads, (((0,), (0,)), ((), ())), preferred_element_type=F32
    )
    small = jnp.concatenate(
        [kernel0.reshape(-1, channels), kernel1.reshape(-1, channels)]
        + [v.reshape(1, channels) for v in (cbias0, cbias1)],
        0,
    )
    bands = lax.axis_size(BANDS)
    piece = -(-small.shape[0] // bands)
    piece += -piece % 16
    small = jnp.pad(small, ((0, piece * bands - small.shape[0]), (0, 0))).astype(BF)
    small = lax.all_to_all(small.reshape(bands, piece, channels), BANDS, 0, 0, tiled=True)
    small = small_whole(small_summed(small, bias_part))
    bands = lax.axis_size("plane") * lax.axis_size("tile")
    total = lax.axis_size("obj") * bands
    weight_grad = scatter_all(
        weight_part.reshape(total, fan // total, -1), (lax.axis_size("obj"), bands)
    )
    return (tok_grad, weight_grad) + small_results(small, conv_kernels.shape[1])


def sent_to_all(array, axes):
    copies = jnp.broadcast_to(array[None], (lax.axis_size(axes),) + array.shape)
    return lax.all_to_all(copies, axes, 0, 0, tiled=True)


def small_summed(parts, bias_part):
    piece = jnp.sum(parts.astype(F32), 0)
    tail = jnp.pad(bias_part[None], ((0, 15), (0, 0)))
    return sent_to_all(jnp.concatenate([piece, tail], 0).astype(BF), "obj")


def small_whole(parts):
    return sent_to_all(jnp.sum(parts.astype(F32), 0).astype(BF), BANDS)


def small_results(parts, per_kernel):
    channels = parts.shape[-1]
    small = parts[:, :-16].reshape(-1, channels).astype(F32)
    bias = jnp.sum(parts[:, -16].astype(F32), 0)
    kernel_grads = small[: 2 * per_kernel].reshape(2, per_kernel, channels)
    return (bias, kernel_grads, small[2 * per_kernel : 2 * per_kernel + 2])


def bits_of(size):
    steps = []
    while size > 1:
        size //= 2
        steps.append(size)
    return steps


def halved(parts, dim, axis, step):
    upper = ((lax.axis_index(axis) // step) % 2).astype(jnp.int32)
    size = lax.axis_size(axis)
    mine = lax.dynamic_slice_in_dim(parts, upper, 1, dim)
    theirs = lax.dynamic_slice_in_dim(parts, 1 - upper, 1, dim)
    other = lax.ppermute(theirs, axis, [(i, i ^ step) for i in range(size)])
    return (mine.astype(F32) + other.astype(F32)).astype(BF)


def near_step():
    return ("plane", 1), 1 + len(bits_of(lax.axis_size("plane"))) - 1


def weight_parts(product):
    fan, columns = product.shape
    objs = lax.axis_size("obj")
    bits = len(bits_of(lax.axis_size("plane"))) + len(bits_of(lax.axis_size("tile")))
    shape = (objs,) + (2,) * bits + (fan // (objs * 2**bits), columns)
    step, dim = near_step()
    return halved(product.astype(BF).reshape(shape), dim, *step)


def weight_scattered(parts):
    objs = parts.shape[0]
    steps = [("plane", s) for s in bits_of(lax.axis_size("plane"))]
    steps += [("tile", s) for s in bits_of(lax.axis_size("tile"))]
    rest = [(i + 1, step) for i, step in enumerate(steps) if i + 1 != near_step()[1]]
    streams = [parts[: objs // 2], parts[objs // 2 :]]
    for one, two in zip(rest, reversed(rest)):
        streams[0] = halved(streams[0], one[0], *one[1])
        streams[1] = halved(streams[1], two[0], *two[1])
    return jnp.concatenate(streams, 0).reshape(objs, *parts.shape[-2:])


def kernel_pass(tokens, gout, deconv_weight, deconv_bias, conv_kernels, conv_biases):
    objects, _, tok_rows, tok_cols, fan = tokens.shape
    _, _, height, breadth, channels = gout.shape
    planes = 3 * objects
    up = height // tok_rows
    edge = 8
    width = breadth + 2 * edge
    extent = height * lax.axis_size("plane")
    row_start = lax.axis_index("plane") * height
    col_start = lax.axis_index("tile") * breadth
    dims = (height, breadth, width)

    tok = tokens.reshape(planes, tok_rows, tok_cols, fan)
    grad_top = gout.reshape(planes, height, breadth, channels)
    flat_tok = lambda array: array.reshape(planes, -1, fan)
    flat_grad = lambda array: array.reshape(planes, -1, channels)

    def columns_beside(bands_of, last):
        def cut(parts):
            cells = [p[:, :, -2:] if last else p[:, :, :2] for p in parts]
            cells = lax.optimization_barrier(cells)
            return jnp.concatenate([c.astype(BF) for c in cells], 1)

        rim = shifted(jnp.stack([cut(parts) for parts in bands_of], 2), "tile", 1 if last else -1)
        room = (edge - 2, 0) if last else (0, edge - 2)
        return flat_grad(jnp.pad(rim, ((0, 0),) * 3 + (room, (0, 0))).astype(F32))

    taps = conv_kernels.reshape(2, 3, 3, channels, channels)
    side = 3 * channels
    ahead = taps[0].transpose(0, 2, 1, 3).reshape(side, side)
    back = taps.transpose(0, 1, 4, 2, 3).reshape(2, side, side)

    flat = lambda rows: (planes, rows * width, channels)
    bands = lax.axis_size(BANDS)
    copies = ((bands, planes, height + breadth, channels), BF, "copies")
    sums = pltpu.VMEM((height + breadth, channels), F32)
    one = ((planes, 1, channels), F32, False)
    prod = lambda rows: pltpu.VMEM((rows * width + 16, side), F32)
    conv_flops = lambda rows: 2 * rows * width * side * side
    mask = pltpu.VMEM((width, channels), F32)

    def contexts(parts, rim, pad, bias, beside):
        parts = lax.all_to_all(parts, BANDS, 0, 0, tiled=True)
        parts, beside = lax.optimization_barrier((parts, beside))
        room = [
            pltpu.VMEM((planes, height + 2 * rim, channels), F32),
            pltpu.VMEM((planes, breadth + 2 * pad, channels), F32),
        ] + [pltpu.VMEM((3, extent + 16, channels), F32)] * 2
        given = [(parts, True), (bias.reshape(1, channels), True)]
        return given, room, lambda kernel: with_contexts(kernel, dims, rim, pad), beside

    rim_rows = ((planes, 4 * breadth, channels), BF, False)
    raw, parts, first, last, cbias1 = call(
        functools.partial(upsample_kernel, (tok_rows, tok_cols, up, height, breadth, channels)),
        planes,
        [(flat_tok(tok), False), (flat_grad(grad_top), False), (deconv_weight, True)],
        [((planes, height * breadth, channels), F32, False), copies, rim_rows, rim_rows, one],
        [sums],
        flops=2 * tok_rows * tok_cols * fan * up * up * channels,
    )
    half = planes // 2
    above, below = shifted(last, "plane", 1), shifted(first, "plane", -1)
    slots = lambda array: array.reshape(planes, 2, 2, breadth, channels)
    beyond = (slots(above), slots(below))
    both = [
        (beyond[0][:, slot], cells, beyond[1][:, slot])
        for slot, cells in enumerate((grad_top, raw.reshape(grad_top.shape)))
    ]
    left, right = columns_beside(both, True), columns_beside(both, False)
    parts, left, right = lax.optimization_barrier((parts, left, right))

    def adjoint_of(first, count):
        kind = (first, -count)
        return call(
            functools.partial(adjoint_kernel, dims),
            count,
            [(flat_grad(grad_top), kind)]
            + [(array, kind) for array in (above, below, left, right)]
            + [(back[1], True)],
            [
                ((count, (height + 4) * width, channels), BF, False),
                ((count, (height + 2) * width, channels), BF, False),
            ],
            [prod(height // 2 + 1)],
            conv_flops(height + 2),
        )

    low = adjoint_of(0, half)
    given, room, wrap, low = contexts(parts, 2, edge, deconv_bias, low)
    act0, slope0, hidden, parts = call(
        wrap(functools.partial(forward_kernel, dims, extent)),
        planes,
        given
        + [(raw, False)]
        + [(array, False) for array in (above, below, left, right)]
        + [(ahead, True)],
        [(flat(height + 4), BF, False)] * 2 + [(flat(height + 2), BF, False), copies],
        [pltpu.VMEM(flat(height + 4)[1:], F32), prod(height // 2 + 1), sums, mask]
        + room,
        conv_flops(height + 2),
    )
    high = adjoint_of(half, planes - half)
    given, room, wrap, high = contexts(parts, 1, edge, deconv_bias + conv_biases[0], high)
    act1, part1, parts = call(
        wrap(functools.partial(middle_kernel, dims, extent, half)),
        planes,
        given
        + [(hidden, False)]
        + [(low[1], (0, half)), (high[1], (half, planes - half))]
        + [(low[0], (0, half)), (high[0], (half, planes - half))],
        [(flat(height + 2), BF, False), (flat(height + 2), BF, False), copies],
        [sums, mask] + room,
    )

    def kernel_gradient_of(act, grad, act_base, grad_base, more=(), rows=9 * channels):
        (result,) = call(
            functools.partial(kernel_grad_kernel, dims, act_base, grad_base),
            planes,
            [(act, False), (grad, False)] + [(array, True) for array in more],
            [((rows, channels), BF, True)],
            [
                pltpu.VMEM((height * width + 16, channels), F32),
                pltpu.VMEM((height * width, side), BF),
                pltpu.VMEM((9 * channels, channels), F32),
            ],
            2 * height * width * side * side,
        )
        return result

    none = jnp.zeros((channels,), F32)
    kernel1 = kernel_gradient_of(act1, flat_grad(grad_top), 0, None)
    given, room, wrap, kernel1 = contexts(parts, 1, edge, none, kernel1)
    gb1, part0, parts, cbias0 = call(
        wrap(functools.partial(backward_kernel, dims, extent)),
        planes,
        given + [(part1, False), (slope0, False), (back[0], True)],
        [(flat(height + 2), BF, False), ((planes, height * breadth, channels), BF, False)]
        + [copies, one],
        [prod(height // 2), sums, mask] + room,
        conv_flops(height),
    )
    piece = -(-(18 * channels + 2) // bands)
    piece += -piece % 16
    more = (kernel1, cbias0, cbias1)
    small = kernel_gradient_of(act0, gb1, 1, 1, more, piece * bands)
    given, room, wrap, small = contexts(parts, 0, 0, none, small)
    small = lax.all_to_all(small.reshape(bands, piece, channels), BANDS, 0, 0, tiled=True)
    tap_grads, bias_part = call(
        wrap(functools.partial(taps_kernel, (height, breadth, up, channels))),
        planes,
        given + [(part0, False)],
        [((planes, tok_rows * tok_cols, up * up * channels), BF, False), one],
        [pltpu.VMEM((height * breadth, channels), F32)] + room,
    )
    tap_grads = tap_grads.reshape(-1, up * up * channels)
    tap_grads, small = lax.optimization_barrier((tap_grads, small))
    product = lax.dot_general(
        tok.reshape(-1, fan), tap_grads, (((0,), (0,)), ((), ())), preferred_element_type=F32
    )
    small = small_summed(small, jnp.sum(bias_part, (0, 1)))
    parts = weight_parts(product)
    tok_grad = lax.dot_general(
        tap_grads, deconv_weight, (((1,), (1,)), ((), ())), preferred_element_type=F32
    )
    tok_grad = tok_grad.astype(BF).reshape(tokens.shape)
    parts, small, tok_grad = lax.optimization_barrier((parts, small, tok_grad))
    small = small_whole(small)
    parts, small = lax.optimization_barrier((weight_scattered(parts), small))
    weight_grad = scattered(parts, "obj")
    return (tok_grad, weight_grad) + small_results(small, conv_kernels.shape[1])


def per_device(tokens, gout, deconv_weight, deconv_bias, conv_kernels, conv_biases):
    channels = gout.shape[-1]
    sizes = [lax.axis_size(axis) for axis in ("obj", "plane", "tile")]
    fits = gout.shape[3] % 16 == 0 and gout.shape[2] % 16 == 0 and channels % 128 == 0
    fits = fits and all(size & (size - 1) == 0 and size > 1 for size in sizes)
    run = kernel_pass if fits else plain_pass
    return run(tokens, gout, deconv_weight, deconv_bias, conv_kernels, conv_biases)


def solution(mesh):
    placed = (
        P("obj", None, "plane", "tile", None),
        P("obj", None, "plane", "tile", None),
        P(),
        P(),
        P(),
        P(),
    )
    return jax.shard_map(
        per_device,
        mesh=mesh,
        in_specs=placed,
        out_specs=(
            P("obj", None, "plane", "tile", None),
            P(EVERY, None),
            P(),
            P(),
            P(),
        ),
        check_vma=False,
    )
```

```python
import functools

import jax
import jax.numpy as jnp
from jax import lax
from jax.experimental import pallas as pl
from jax.experimental.pallas import tpu as pltpu
from jax.sharding import PartitionSpec as P

BANDS = ("plane", "tile")
EVERY = ("obj", "plane", "tile")
CONV_DIMS = ("NHWC", "HWIO", "NHWC")
BF = jnp.bfloat16
F32 = jnp.float32


def shifted(array, axis, step):
    size = lax.axis_size(axis)
    pairs = [(i, i + step) for i in range(size) if 0 <= i + step < size]
    return lax.ppermute(array, axis, pairs)


def grow_dim(tok, grad, axis, dim, tok_rim, grad_rim):
    planes, lanes = tok.shape[0], grad.shape[-1]

    def cut(array, rim, last):
        length = array.shape[dim]
        start = length - rim if last else 0
        return lax.slice_in_dim(array, start, start + rim, axis=dim)

    def pack(last):
        parts = [cut(tok, tok_rim, last), cut(grad, grad_rim, last)]
        return jnp.concatenate([part.reshape(planes, -1, lanes) for part in parts], 1)

    def unpack(packed):
        shapes = [cut(tok, tok_rim, False).shape, cut(grad, grad_rim, False).shape]
        rows = shapes[0][1] * shapes[0][2] * shapes[0][3] // lanes
        return packed[:, :rows].reshape(shapes[0]), packed[:, rows:].reshape(shapes[1])

    before = unpack(shifted(pack(True), axis, 1))
    after = unpack(shifted(pack(False), axis, -1))
    return [
        jnp.concatenate([low, mid, high], axis=dim)
        for low, mid, high in zip(before, (tok, grad), after)
    ]


def band_sums(rows, cols):
    height = rows.shape[1]

    def joined(own, other, axis, step):
        upper = (lax.axis_index(axis) & step) != 0
        return jnp.where(
            upper, jnp.concatenate([other, own], 1), jnp.concatenate([own, other], 1)
        )

    rows, cols = rows.astype(BF), cols.astype(BF)
    for axis in ("tile", "plane"):
        size, step = lax.axis_size(axis), 1
        while step < size:
            height = rows.shape[1]
            other = lax.ppermute(
                jnp.concatenate([rows, cols], 1), axis, [(i, i ^ step) for i in range(size)]
            )
            other_rows, other_cols = other[:, :height], other[:, height:]
            if axis == "tile":
                rows = (rows.astype(F32) + other_rows.astype(F32)).astype(BF)
                cols = joined(cols, other_cols, axis, step)
            else:
                rows = joined(rows, other_rows, axis, step)
                cols = (cols.astype(F32) + other_cols.astype(F32)).astype(BF)
            step *= 2
    return rows.astype(F32), cols.astype(F32)


def spread(row_sum, col_sum, extent, ring, row_start, col_start, height, breadth):
    planes, _, channels = row_sum.shape
    rows = row_sum.reshape(planes // 3, 3, extent, channels) / extent
    cols = col_sum.reshape(planes // 3, 3, extent, channels) / extent
    row_ctx = jnp.stack([rows[:, 1], rows[:, 0], cols[:, 0]], 1)
    col_ctx = jnp.stack([rows[:, 2], cols[:, 2], cols[:, 1]], 1)

    def band(ctx, start, length):
        ctx = jnp.pad(ctx, ((0, 0), (0, 0), (ring, ring), (0, 0)))
        ctx = lax.dynamic_slice_in_dim(ctx, start, length + 2 * ring, 2)
        return ctx.reshape(planes, length + 2 * ring, channels)

    row_band = band(row_ctx, row_start, height)
    col_band = band(col_ctx, col_start, breadth)
    return row_band[:, :, None, :] + col_band[:, None, :, :]


def inside(ring, extent, row_start, col_start, height, breadth):
    row = row_start - ring + lax.iota(jnp.int32, height + 2 * ring)
    col = col_start - ring + lax.iota(jnp.int32, breadth + 2 * ring)
    row_ok = (row >= 0) & (row < extent)
    col_ok = (col >= 0) & (col < extent)
    return (row_ok[:, None] & col_ok[None, :])[None, :, :, None]


def conv(padded, kernel):
    return lax.conv_general_dilated(
        padded, kernel, (1, 1), "VALID", dimension_numbers=CONV_DIMS, preferred_element_type=F32
    )


def kernel_gradient(padded, grad):
    return lax.conv_general_dilated(
        padded,
        grad,
        (1, 1),
        "VALID",
        dimension_numbers=("CHWN", "IHWO", "HWNC"),
        preferred_element_type=F32,
    )


def trim(array, ring):
    return array[:, ring:-ring, ring:-ring, :]


def slope(pre):
    sig = jax.nn.sigmoid(pre)
    return sig * (1.0 + pre * (1.0 - sig))


def scattered(parts, axes):
    return jnp.sum(lax.all_to_all(parts, axes, 0, 0, tiled=True).astype(F32), 0)


def scatter_all(blocks, sizes):
    objs, bands = sizes
    blocks = blocks.astype(BF).reshape((objs, bands) + blocks.shape[1:])
    blocks = jnp.moveaxis(blocks, 1, 0)
    part = scattered(blocks, BANDS).astype(BF)
    return scattered(part, "obj")


def call(kernel, planes, ins, outs, scratch=(), flops=0):
    def spec(shape, kind):
        rest = (0,) * (len(shape) - 1)
        if kind is True:
            return pl.BlockSpec(shape, lambda p: (0,) + rest)
        if kind == "copies":
            return pl.BlockSpec(
                (shape[0], None) + shape[2:], lambda p: (0, p) + (0,) * (len(shape) - 2)
            )
        if kind is False:
            return pl.BlockSpec((None,) + shape[1:], lambda p: (p,) + rest)
        first, count = kind
        if count < 0:
            return pl.BlockSpec((None,) + shape[1:], lambda p: (p + first,) + rest)
        return pl.BlockSpec(
            (None,) + shape[1:], lambda p: (jnp.clip(p - first, 0, count - 1),) + rest
        )

    moved = sum(a.size * a.dtype.itemsize for a, _ in ins)
    return pl.pallas_call(
        kernel,
        grid=(planes,),
        in_specs=[spec(a.shape, kind) for a, kind in ins],
        out_specs=[spec(shape, kind) for shape, _, kind in outs],
        out_shape=[jax.ShapeDtypeStruct(shape, dtype) for shape, dtype, _ in outs],
        scratch_shapes=list(scratch),
        compiler_params=pltpu.CompilerParams(
            dimension_semantics=("arbitrary",), vmem_limit_bytes=60 << 20
        ),
        cost_estimate=pl.CostEstimate(
            flops=flops * planes, bytes_accessed=2 * moved, transcendentals=0
        ),
    )(*[a for a, _ in ins])


def inside_limits(ring, extent, height, breadth, width):
    row_start = lax.axis_index("plane") * height
    col_start = lax.axis_index("tile") * breadth
    edge = (width - breadth) // 2
    column = lax.broadcasted_iota(jnp.int32, (width, 128), 0) - edge
    ok = (column >= -ring) & (column < breadth + ring)
    ok = ok & (col_start + column >= 0) & (col_start + column < extent)
    ones = jnp.where(ok, 1.0, 0.0)

    def limit(r):
        row = row_start + r - ring
        return jnp.where((row >= 0) & (row < extent), 0.5, 2.0)

    return ones, limit


def span(row, width, rows=1):
    return pl.ds(pl.multiple_of(row * width, 16), rows * width)


def span8(start, size):
    return pl.ds(pl.multiple_of(start, 8), size)


def loop(rows, body, carry=None, unroll=4):
    return lax.fori_loop(0, rows, body, carry, unroll=unroll)


def convolve_rows(
    src, base, kernel_ref, prod, pair, rows_out, width, chunks, finish, carry, flipped=False
):
    step = rows_out // chunks
    pairs = step // 2
    size = pairs * width
    order = (2, 1, 0) if flipped else (0, 1, 2)
    channels = kernel_ref.shape[0] // 3
    side = 3 * channels

    @pl.when(pl.program_id(0) == 0)
    def _():
        pair[...] = jnp.zeros(pair.shape, BF)
        for row in range(2):
            for tap, dy in enumerate(order):
                at = (row + dy) * channels
                pair[at : at + channels, row * side : (row + 1) * side] = kernel_ref[
                    tap * channels : (tap + 1) * channels, :
                ]

    def chunk(index, carry):
        start = base + index * step

        def lane(j):
            block = src[span(start + j // 2 * 2, width, step), :]
            block = block.reshape(pairs, 2 * width, channels)
            return block[:, j % 2 * width : (j % 2 + 1) * width].reshape(size, channels)

        lhs = jnp.concatenate([lane(j) for j in range(4)], 1)
        prod[pl.ds(8, size), :] = jnp.dot(lhs, pair[...], preferred_element_type=F32)
        first, _, last = order

        def rows(q, carry):
            view = prod.at[span8(q * width, width + 16), :]
            for row in range(2):
                at = row * side
                value = (
                    view[7 + first : 7 + first + width, at : at + channels]
                    + view[8 : 8 + width, at + channels : at + 2 * channels]
                    + view[7 + last : 7 + last + width, at + 2 * channels : at + side]
                )
                carry = finish(index * step + 2 * q + row, value, carry)
            return carry

        return loop(pairs, rows, carry, unroll=2)

    return lax.fori_loop(0, chunks, chunk, carry)


def send_sums(sums, copies_ref):
    for copy in range(copies_ref.shape[0]):
        copies_ref[copy] = sums[...].astype(BF)


def place_row(rows, r, slot, center, left_ref, right_ref):
    side = left_ref.shape[0] // rows // 2
    at = span8((2 * r + slot) * side, side)
    return jnp.concatenate([left_ref[at, :], center, right_ref[at, :]], 0)


def place_rows(rows, breadth, slot, refs, put):
    own_ref, above_ref, below_ref, left_ref, right_ref = refs

    def one(r, ref, at):
        center = ref[at, :].astype(F32)
        put(r, place_row(rows, r, slot, center, left_ref, right_ref))

    for r in range(2):
        at = (2 * slot + r) * breadth
        one(r, above_ref, slice(at, at + breadth))
        one(rows - 2 + r, below_ref, slice(at, at + breadth))

    def inner(r, carry):
        one(r + 2, own_ref, span(r, breadth))
        return carry

    loop(rows - 4, inner, 0)


def upsample_kernel(
    dims, tok_ref, grad_ref, weight_ref,
    raw_ref, copies_ref, first_ref, last_ref, bias_ref, sums,
):
    tok_rows, tok_cols, up, height, breadth, channels = dims
    cut = up * channels
    for a in range(up):
        weight = weight_ref[:, a * cut : (a + 1) * cut]
        prod = jnp.dot(tok_ref[...], weight, preferred_element_type=F32)
        for b in range(up):
            for i in range(tok_rows):
                raw_ref[pl.ds((up * i + a) * breadth + b, tok_cols, stride=up), :] = prod[
                    i * tok_cols : (i + 1) * tok_cols, b * channels : (b + 1) * channels
                ]

    def add(r, total):
        own = raw_ref[span(r, breadth), :]
        sums[pl.ds(r, 1), :] = jnp.sum(own, 0, keepdims=True)
        total, bias = total
        return total + own, bias + grad_ref[span(r, breadth), :].astype(F32)

    zero = jnp.zeros((breadth, channels), F32)
    total, bias = loop(height, add, (zero, zero))
    sums[pl.ds(height, breadth), :] = total
    bias_ref[...] = jnp.sum(bias, 0, keepdims=True)
    send_sums(sums, copies_ref)
    rim = 2 * breadth
    tail = slice((height - 2) * breadth, height * breadth)
    for ref, at in ((first_ref, slice(0, rim)), (last_ref, tail)):
        ref[:rim, :] = grad_ref[at, :]
        ref[rim:, :] = raw_ref[at, :].astype(BF)


def forward_kernel(
    dims, extent, row_ref, col_ref, own_ref, above_ref, below_ref, left_ref, right_ref, kernel_ref,
    act_ref, slope_ref, next_ref, copies_ref, raw_ref, prod, pair, sums_ref, mask,
):
    height, breadth, width = dims
    mask[...], limit = inside_limits(2, extent, height, breadth, width)
    edge = (width - breadth) // 2

    def activate(r, value):
        raw_ref[span(r, width), :] = value
        pre = value + row_ref[pl.ds(r, 1), :] + col_ref[...]
        sig = 0.5 * jnp.tanh(0.5 * pre) + 0.5
        ok = mask[...] > limit(r)
        act = pre * sig
        act_ref[span(r, width), :] = jnp.where(ok, act, 0.0).astype(BF)
        slope_ref[span(r, width), :] = (sig + act * (1.0 - sig)).astype(BF)

    refs = (own_ref, above_ref, below_ref, left_ref, right_ref)
    place_rows(height + 4, breadth, 1, refs, activate)
    zero = jnp.zeros((breadth, sums_ref.shape[1]), F32)

    def finish(r, value, total):
        value = raw_ref[span(r + 1, width), :] + value
        next_ref[span(r, width), :] = value.astype(BF)
        own = value[edge : edge + breadth]
        inner = (r >= 1) & (r <= height)

        @pl.when(inner)
        def _():
            sums_ref[pl.ds(r - 1, 1), :] = jnp.sum(own, 0, keepdims=True)

        return total + jnp.where(inner, own, 0.0)

    sums_ref[pl.ds(height, breadth), :] = convolve_rows(
        act_ref, 0, kernel_ref, prod, pair, height + 2, width, 1, finish, zero
    )
    send_sums(sums_ref, copies_ref)


def adjoint_kernel(
    dims, own_ref, above_ref, below_ref, left_ref, right_ref, kernel_ref, wide_ref, out_ref, prod, pair
):
    height, breadth, width = dims

    def put(r, row):
        wide_ref[span(r, width), :] = row.astype(BF)

    refs = (own_ref, above_ref, below_ref, left_ref, right_ref)
    place_rows(height + 4, breadth, 0, refs, put)

    def finish(r, value, carry):
        out_ref[span(r, width), :] = value.astype(BF)
        return carry

    convolve_rows(wide_ref, 0, kernel_ref, prod, pair, height + 2, width, 1, finish, 0, True)


def context_kernel(dims, ring, side, parts_ref, bias_ref, row_ref, col_ref, rows, cols):
    height, breadth, _ = dims
    bands, planes = parts_ref.shape[:2]
    extent = rows.shape[1] - 16
    down, across = extent // height, extent // breadth
    rows[...] = jnp.zeros(rows.shape, F32)
    cols[...] = jnp.zeros(cols.shape, F32)
    scale = 1.0 / extent
    for first in range(0, planes, 3):
        for q in range(3):
            part = lambda p, t, at, size: parts_ref[p * across + t, first + q, at : at + size, :].astype(F32)
            for p in range(down):
                pieces = [part(p, t, 0, height) for t in range(across)]
                rows[q, 8 + p * height : 8 + (p + 1) * height, :] = scale * sum(pieces)
            for t in range(across):
                pieces = [part(p, t, height, breadth) for p in range(down)]
                cols[q, 8 + t * breadth : 8 + (t + 1) * breadth, :] = scale * sum(pieces)
        row_at = span8(lax.axis_index("plane") * height, height + 16)
        col_at = span8(lax.axis_index("tile") * breadth, breadth + 16)
        for q, (ref, other) in enumerate(((rows, 1), (rows, 0), (cols, 0))):
            view = ref.at[other, row_at, :]
            row_ref[first + q] = view[8 - ring : 8 + height + ring, :] + 2.0 * bias_ref[...]
        for q, (ref, other) in enumerate(((rows, 2), (cols, 2), (cols, 1))):
            view = ref.at[other, col_at, :]
            col_ref[first + q] = view[8 - side : 8 + breadth + side, :] + bias_ref[...]


def with_contexts(kernel, dims, ring, side):
    def body(parts_ref, bias_ref, *refs):
        row_all, col_all, rows, cols = refs[-4:]

        @pl.when(pl.program_id(0) == 0)
        def _():
            context_kernel(
                dims, ring, side, parts_ref, bias_ref, row_all, col_all, rows, cols
            )

        plane = pl.program_id(0)
        kernel(row_all.at[plane], col_all.at[plane], *refs[:-4])

    return body


def middle_kernel(
    dims, extent, half, row_ref, col_ref, hid_ref, adj_low, adj_high, grad_low, grad_high, act_ref, next_ref, copies_ref, sums_ref, mask,
):
    height, breadth, width = dims
    mask[...], limit = inside_limits(1, extent, height, breadth, width)
    low = pl.program_id(0) < half
    edge = (width - breadth) // 2

    def one(r, total):
        pre = hid_ref[span(r, width), :].astype(F32) + row_ref[pl.ds(r, 1), :] + col_ref[...]
        sig = 0.5 * jnp.tanh(0.5 * pre) + 0.5
        ok = mask[...] > limit(r)
        act = pre * sig
        act_ref[span(r, width), :] = jnp.where(ok, act, 0.0).astype(BF)
        here, after = span(r, width), span(r + 1, width)
        adj = jnp.where(low, adj_low[here, :].astype(F32), adj_high[here, :].astype(F32))
        grad = jnp.where(low, grad_low[after, :].astype(F32), grad_high[after, :].astype(F32))
        dz = adj * (sig + act * (1.0 - sig))
        next_ref[here, :] = (grad + dz).astype(BF)
        own = dz[edge : edge + breadth]
        inner = (r >= 1) & (r <= height)

        @pl.when(inner)
        def _():
            sums_ref[pl.ds(r - 1, 1), :] = jnp.sum(own, 0, keepdims=True)

        return total + jnp.where(inner, own, 0.0)

    sums_ref[pl.ds(height, breadth), :] = loop(height + 2, one, jnp.zeros((breadth, sums_ref.shape[1]), F32))
    send_sums(sums_ref, copies_ref)


def backward_kernel(
    dims, extent, row_ref, col_ref, part_ref, slope_ref, kernel_ref,
    grad_ref, next_ref, copies_ref, bias_ref, prod, pair, sums_ref, mask,
):
    height, breadth, width = dims
    mask[...], limit = inside_limits(1, extent, height, breadth, width)
    edge = (width - breadth) // 2

    def full(r):
        return part_ref[span(r, width), :].astype(F32) + row_ref[pl.ds(r, 1), :] + col_ref[...]

    def round_row(r, carry):
        ok = mask[...] > limit(r)
        grad_ref[span(r, width), :] = jnp.where(ok, full(r), 0.0).astype(BF)
        return carry

    loop(height + 2, round_row, 0)
    zero = jnp.zeros((breadth, sums_ref.shape[1]), F32)

    def finish(r, value, carry):
        total, bias = carry
        dz = value * slope_ref[span(r + 2, width), :].astype(F32)
        own = dz[edge : edge + breadth]
        grad = full(r + 1)[edge : edge + breadth]
        sums_ref[pl.ds(r, 1), :] = jnp.sum(own, 0, keepdims=True)
        next_ref[pl.ds(pl.multiple_of(r * breadth, 16), breadth), :] = (grad + own).astype(BF)
        return total + own, bias + grad

    total, bias = convolve_rows(
        grad_ref, 0, kernel_ref, prod, pair, height, width, 1, finish, (zero, zero), True
    )
    sums_ref[pl.ds(height, breadth), :] = total
    send_sums(sums_ref, copies_ref)
    bias_ref[...] = jnp.sum(bias, 0, keepdims=True)


def taps_kernel(dims, row_ref, col_ref, part_ref, tap_ref, bias_ref, full):
    height, breadth, up, channels = dims

    def one(r, total):
        at = pl.ds(pl.multiple_of(r * breadth, 16), breadth)
        value = part_ref[at, :].astype(F32) + row_ref[pl.ds(r, 1), :] + col_ref[...]
        full[at, :] = value
        return total + value

    total = loop(height, one, jnp.zeros(col_ref.shape, F32))
    bias_ref[...] = jnp.sum(total, 0, keepdims=True)
    tok_cols = breadth // up
    for i in range(height // up):
        for a in range(up):
            for b in range(up):
                piece = full[pl.ds((up * i + a) * breadth + b, tok_cols, stride=up), :]
                tap = a * up + b
                tap_ref[
                    i * tok_cols : (i + 1) * tok_cols, tap * channels : (tap + 1) * channels
                ] = piece.astype(BF)


def kernel_grad_kernel(dims, act_base, grad_base, act_ref, grad_ref, *refs):
    more, (rounded_ref, wide, moved, out_ref) = refs[:-4], refs[-4:]

    height, breadth, width = dims
    edge = (width - breadth) // 2
    channels = act_ref.shape[1]
    column = lax.broadcasted_iota(jnp.int32, (width, channels), 0)
    ok = (column >= edge) & (column < edge + breadth)
    wide[pl.ds(0, 8), :] = jnp.zeros((8, channels), F32)
    wide[pl.ds(8 + height * width, 8), :] = jnp.zeros((8, channels), F32)

    def fill(r, carry):
        if grad_base is None:
            value = grad_ref[span(r, breadth), :].astype(F32)
            rim = jnp.zeros((edge, channels), F32)
            value = jnp.concatenate([rim, value, rim], 0)
        else:
            value = jnp.where(ok, grad_ref[span(r + grad_base, width), :].astype(F32), 0.0)
        wide[span8(r * width + 8, width), :] = value
        return carry

    loop(height, fill, 0)

    def move(r, carry):
        view = wide.at[span8(r * width, width + 16), :]
        for dx in range(3):
            moved[span(r, width), dx * channels : (dx + 1) * channels] = view[
                9 - dx : 9 - dx + width, :
            ].astype(BF)
        return carry

    loop(height, move, 0)

    @pl.when(pl.program_id(0) == 0)
    def _():
        out_ref[...] = jnp.zeros(out_ref.shape, F32)

    chunks = 2
    step = height // chunks

    def chunk(index, carry):
        start = index * step
        lhs = jnp.concatenate(
            [act_ref[span(start + act_base + dy, width, step), :] for dy in range(3)], 1
        )
        result = lax.dot_general(
            lhs,
            moved[span(start, width, step), :],
            (((0,), (0,)), ((), ())),
            preferred_element_type=F32,
        )
        for tap in range(9):
            dy, dx = divmod(tap, 3)
            out_ref[tap * channels : (tap + 1) * channels, :] += result[
                dy * channels : (dy + 1) * channels, dx * channels : (dx + 1) * channels
            ]
        return carry

    lax.fori_loop(0, chunks, chunk, 0)

    @pl.when(pl.program_id(0) == pl.num_programs(0) - 1)
    def _():
        size = out_ref.shape[0]
        rounded_ref[:size, :] = out_ref[...].astype(BF)
        if more:
            other_ref, bias0_ref, bias1_ref = more
            rounded_ref[size : 2 * size, :] = other_ref[...]
            tail = rounded_ref.shape[0] - 2 * size
            row = lax.broadcasted_iota(jnp.int32, (tail, channels), 0)
            bias0 = jnp.sum(bias0_ref[...], 0)
            bias1 = jnp.sum(bias1_ref[...], 0)
            value = jnp.where(row == 0, bias0, jnp.where(row == 1, bias1, 0.0))
            rounded_ref[2 * size :, :] = value.astype(BF)


def plain_pass(tokens, gout, deconv_weight, deconv_bias, conv_kernels, conv_biases):
    objects, _, tok_rows, tok_cols, fan = tokens.shape
    _, _, height, breadth, channels = gout.shape
    planes = 3 * objects
    up = height // tok_rows
    extent = height * lax.axis_size("plane")
    row_start = lax.axis_index("plane") * height
    col_start = lax.axis_index("tile") * breadth
    place = (extent, row_start, col_start, height, breadth)
    ctx_place = (row_start, col_start, height, breadth)

    tok = tokens.reshape(planes, tok_rows, tok_cols, fan)
    grad_top = gout.reshape(planes, height, breadth, channels)
    tok_wide, grad_wide = grow_dim(tok, grad_top, "plane", 1, 1, 2)
    tok_wide, grad_wide = grow_dim(tok_wide, grad_wide, "tile", 2, 1, 2)

    taps = conv_kernels.reshape(2, 3, 3, channels, channels)
    back = taps[:, ::-1, ::-1].transpose(0, 1, 2, 4, 3)

    raw = jnp.dot(tok_wide.reshape(-1, fan), deconv_weight, preferred_element_type=F32)
    raw = raw.reshape(planes, tok_rows + 2, tok_cols + 2, up, up, channels)
    raw = raw.transpose(0, 1, 3, 2, 4, 5)
    raw = raw.reshape(planes, up * (tok_rows + 2), up * (tok_cols + 2), channels)
    raw = trim(raw, up - 2)

    own = trim(raw, 2)
    row0, col0 = band_sums(jnp.sum(own, 2), jnp.sum(own, 1))
    bias = deconv_bias
    pre0 = raw + bias + spread(
        row0 + extent * bias, col0 + extent * bias, extent, 2, *ctx_place
    )
    act0 = jnp.where(inside(2, *place), jax.nn.silu(pre0), 0.0).astype(BF)
    step0 = conv(act0, taps[0])

    own = trim(step0, 1)
    row1, col1 = band_sums(jnp.sum(own, 2), jnp.sum(own, 1))
    bias = deconv_bias + conv_biases[0]
    pre1 = trim(raw, 1) + step0 + bias + spread(
        row0 + row1 + extent * bias, col0 + col1 + extent * bias, extent, 1, *ctx_place
    )
    ok1 = inside(1, *place)
    act1 = jnp.where(ok1, jax.nn.silu(pre1), 0.0).astype(BF)

    dz1 = conv(grad_wide, back[1]) * slope(pre1)
    own = trim(dz1, 1)
    drow1, dcol1 = band_sums(jnp.sum(own, 2), jnp.sum(own, 1))
    kernel1 = kernel_gradient(act1, grad_top)
    cbias1 = jnp.sum(grad_top.astype(F32), (0, 1, 2))
    grad1 = trim(grad_wide, 1).astype(F32) + dz1 + spread(drow1, dcol1, extent, 1, *ctx_place)
    gb1 = jnp.where(ok1, grad1, 0.0).astype(BF)
    own1 = trim(grad1, 1)
    cbias0 = jnp.sum(own1, (0, 1, 2))

    dz0 = conv(gb1, back[0]) * slope(trim(pre0, 2))
    drow0, dcol0 = band_sums(jnp.sum(dz0, 2), jnp.sum(dz0, 1))
    kernel0 = kernel_gradient(trim(act0, 1), trim(gb1, 1))
    grad0 = own1 + dz0 + spread(drow0, dcol0, extent, 0, *ctx_place)
    bias_part = jnp.sum(grad0, (0, 1, 2))

    gb0 = grad0.astype(BF).reshape(planes, tok_rows, up, tok_cols, up, channels)
    tap_grads = gb0.transpose(0, 1, 3, 2, 4, 5).reshape(-1, up * up * channels)
    tok_grad = lax.dot_general(
        tap_grads, deconv_weight, (((1,), (1,)), ((), ())), preferred_element_type=F32
    )
    tok_grad = tok_grad.astype(BF).reshape(tokens.shape)
    weight_part = lax.dot_general(
        tok.reshape(-1, fan), tap_grads, (((0,), (0,)), ((), ())), preferred_element_type=F32
    )
    small = jnp.concatenate(
        [kernel0.reshape(-1, channels), kernel1.reshape(-1, channels)]
        + [v.reshape(1, channels) for v in (cbias0, cbias1)],
        0,
    )
    bands = lax.axis_size(BANDS)
    piece = -(-small.shape[0] // bands)
    piece += -piece % 16
    small = jnp.pad(small, ((0, piece * bands - small.shape[0]), (0, 0))).astype(BF)
    small = lax.all_to_all(small.reshape(bands, piece, channels), BANDS, 0, 0, tiled=True)
    small = small_whole(small_summed(small, bias_part))
    bands = lax.axis_size("plane") * lax.axis_size("tile")
    total = lax.axis_size("obj") * bands
    weight_grad = scatter_all(
        weight_part.reshape(total, fan // total, -1), (lax.axis_size("obj"), bands)
    )
    return (tok_grad, weight_grad) + small_results(small, conv_kernels.shape[1])


def sent_to_all(array, axes):
    copies = jnp.broadcast_to(array[None], (lax.axis_size(axes),) + array.shape)
    return lax.all_to_all(copies, axes, 0, 0, tiled=True)


def small_summed(parts, bias_part):
    piece = jnp.sum(parts.astype(F32), 0)
    tail = jnp.pad(bias_part[None], ((0, 15), (0, 0)))
    return sent_to_all(jnp.concatenate([piece, tail], 0).astype(BF), "obj")


def small_whole(parts):
    return sent_to_all(jnp.sum(parts.astype(F32), 0).astype(BF), BANDS)


def small_results(parts, per_kernel):
    channels = parts.shape[-1]
    small = parts[:, :-16].reshape(-1, channels).astype(F32)
    bias = jnp.sum(parts[:, -16].astype(F32), 0)
    kernel_grads = small[: 2 * per_kernel].reshape(2, per_kernel, channels)
    return (bias, kernel_grads, small[2 * per_kernel : 2 * per_kernel + 2])


def bits_of(size):
    steps = []
    while size > 1:
        size //= 2
        steps.append(size)
    return steps


def halved(parts, dim, axis, step):
    upper = ((lax.axis_index(axis) // step) % 2).astype(jnp.int32)
    size = lax.axis_size(axis)
    mine = lax.dynamic_slice_in_dim(parts, upper, 1, dim)
    theirs = lax.dynamic_slice_in_dim(parts, 1 - upper, 1, dim)
    other = lax.ppermute(theirs, axis, [(i, i ^ step) for i in range(size)])
    return (mine.astype(F32) + other.astype(F32)).astype(BF)


def near_step():
    return ("plane", 1), 1 + len(bits_of(lax.axis_size("plane"))) - 1


def weight_parts(product):
    fan, columns = product.shape
    objs = lax.axis_size("obj")
    bits = len(bits_of(lax.axis_size("plane"))) + len(bits_of(lax.axis_size("tile")))
    shape = (objs,) + (2,) * bits + (fan // (objs * 2**bits), columns)
    step, dim = near_step()
    return halved(product.astype(BF).reshape(shape), dim, *step)


def weight_scattered(parts):
    objs = parts.shape[0]
    steps = [("plane", s) for s in bits_of(lax.axis_size("plane"))]
    steps += [("tile", s) for s in bits_of(lax.axis_size("tile"))]
    rest = [(i + 1, step) for i, step in enumerate(steps) if i + 1 != near_step()[1]]
    streams = [parts[: objs // 2], parts[objs // 2 :]]
    for one, two in zip(rest, reversed(rest)):
        streams[0] = halved(streams[0], one[0], *one[1])
        streams[1] = halved(streams[1], two[0], *two[1])
    return jnp.concatenate(streams, 0).reshape(objs, *parts.shape[-2:])


def kernel_pass(tokens, gout, deconv_weight, deconv_bias, conv_kernels, conv_biases):
    objects, _, tok_rows, tok_cols, fan = tokens.shape
    _, _, height, breadth, channels = gout.shape
    planes = 3 * objects
    up = height // tok_rows
    edge = 8
    width = breadth + 2 * edge
    extent = height * lax.axis_size("plane")
    row_start = lax.axis_index("plane") * height
    col_start = lax.axis_index("tile") * breadth
    dims = (height, breadth, width)

    tok = tokens.reshape(planes, tok_rows, tok_cols, fan)
    grad_top = gout.reshape(planes, height, breadth, channels)
    flat_tok = lambda array: array.reshape(planes, -1, fan)
    flat_grad = lambda array: array.reshape(planes, -1, channels)

    def columns_beside(bands_of, last):
        def cut(parts):
            cells = [p[:, :, -2:] if last else p[:, :, :2] for p in parts]
            cells = lax.optimization_barrier(cells)
            return jnp.concatenate([c.astype(BF) for c in cells], 1)

        rim = shifted(jnp.stack([cut(parts) for parts in bands_of], 2), "tile", 1 if last else -1)
        room = (edge - 2, 0) if last else (0, edge - 2)
        return flat_grad(jnp.pad(rim, ((0, 0),) * 3 + (room, (0, 0))).astype(F32))

    taps = conv_kernels.reshape(2, 3, 3, channels, channels)
    side = 3 * channels
    ahead = taps[0].transpose(0, 2, 1, 3).reshape(side, side)
    back = taps.transpose(0, 1, 4, 2, 3).reshape(2, side, side)

    flat = lambda rows: (planes, rows * width, channels)
    bands = lax.axis_size(BANDS)
    copies = ((bands, planes, height + breadth, channels), BF, "copies")
    sums = pltpu.VMEM((height + breadth, channels), F32)
    one = ((planes, 1, channels), F32, False)
    prod = lambda rows: [
        pltpu.VMEM((rows // 2 * width + 16, 2 * side), F32),
        pltpu.VMEM((4 * channels, 2 * side), BF),
    ]
    conv_flops = lambda rows: 2 * rows * width * side * side
    mask = pltpu.VMEM((width, channels), F32)

    def contexts(parts, rim, pad, bias, beside):
        parts = lax.all_to_all(parts, BANDS, 0, 0, tiled=True)
        parts, beside = lax.optimization_barrier((parts, beside))
        room = [
            pltpu.VMEM((planes, height + 2 * rim, channels), F32),
            pltpu.VMEM((planes, breadth + 2 * pad, channels), F32),
        ] + [pltpu.VMEM((3, extent + 16, channels), F32)] * 2
        given = [(parts, True), (bias.reshape(1, channels), True)]
        return given, room, lambda kernel: with_contexts(kernel, dims, rim, pad), beside

    rim_rows = ((planes, 4 * breadth, channels), BF, False)
    raw, parts, first, last, cbias1 = call(
        functools.partial(upsample_kernel, (tok_rows, tok_cols, up, height, breadth, channels)),
        planes,
        [(flat_tok(tok), False), (flat_grad(grad_top), False), (deconv_weight, True)],
        [((planes, height * breadth, channels), F32, False), copies, rim_rows, rim_rows, one],
        [sums],
        flops=2 * tok_rows * tok_cols * fan * up * up * channels,
    )
    half = planes // 2
    above, below = shifted(last, "plane", 1), shifted(first, "plane", -1)
    slots = lambda array: array.reshape(planes, 2, 2, breadth, channels)
    beyond = (slots(above), slots(below))
    both = [
        (beyond[0][:, slot], cells, beyond[1][:, slot])
        for slot, cells in enumerate((grad_top, raw.reshape(grad_top.shape)))
    ]
    left, right = columns_beside(both, True), columns_beside(both, False)
    parts, left, right = lax.optimization_barrier((parts, left, right))

    def adjoint_of(first, count):
        kind = (first, -count)
        return call(
            functools.partial(adjoint_kernel, dims),
            count,
            [(flat_grad(grad_top), kind)]
            + [(array, kind) for array in (above, below, left, right)]
            + [(back[1], True)],
            [
                ((count, (height + 4) * width, channels), BF, False),
                ((count, (height + 2) * width, channels), BF, False),
            ],
            prod(height + 2),
            conv_flops(height + 2),
        )

    low = adjoint_of(0, half)
    given, room, wrap, low = contexts(parts, 2, edge, deconv_bias, low)
    act0, slope0, hidden, parts = call(
        wrap(functools.partial(forward_kernel, dims, extent)),
        planes,
        given
        + [(raw, False)]
        + [(array, False) for array in (above, below, left, right)]
        + [(ahead, True)],
        [(flat(height + 4), BF, False)] * 2 + [(flat(height + 2), BF, False), copies],
        [pltpu.VMEM(flat(height + 4)[1:], F32), *prod(height + 2), sums, mask]
        + room,
        conv_flops(height + 2),
    )
    high = adjoint_of(half, planes - half)
    given, room, wrap, high = contexts(parts, 1, edge, deconv_bias + conv_biases[0], high)
    act1, part1, parts = call(
        wrap(functools.partial(middle_kernel, dims, extent, half)),
        planes,
        given
        + [(hidden, False)]
        + [(low[1], (0, half)), (high[1], (half, planes - half))]
        + [(low[0], (0, half)), (high[0], (half, planes - half))],
        [(flat(height + 2), BF, False), (flat(height + 2), BF, False), copies],
        [sums, mask] + room,
    )

    def kernel_gradient_of(act, grad, act_base, grad_base, more=(), rows=9 * channels):
        (result,) = call(
            functools.partial(kernel_grad_kernel, dims, act_base, grad_base),
            planes,
            [(act, False), (grad, False)] + [(array, True) for array in more],
            [((rows, channels), BF, True)],
            [
                pltpu.VMEM((height * width + 16, channels), F32),
                pltpu.VMEM((height * width, side), BF),
                pltpu.VMEM((9 * channels, channels), F32),
            ],
            2 * height * width * side * side,
        )
        return result

    none = jnp.zeros((channels,), F32)
    kernel1 = kernel_gradient_of(act1, flat_grad(grad_top), 0, None)
    given, room, wrap, kernel1 = contexts(parts, 1, edge, none, kernel1)
    gb1, part0, parts, cbias0 = call(
        wrap(functools.partial(backward_kernel, dims, extent)),
        planes,
        given + [(part1, False), (slope0, False), (back[0], True)],
        [(flat(height + 2), BF, False), ((planes, height * breadth, channels), BF, False)]
        + [copies, one],
        [*prod(height), sums, mask] + room,
        conv_flops(height),
    )
    piece = -(-(18 * channels + 2) // bands)
    piece += -piece % 16
    more = (kernel1, cbias0, cbias1)
    small = kernel_gradient_of(act0, gb1, 1, 1, more, piece * bands)
    given, room, wrap, small = contexts(parts, 0, 0, none, small)
    small = lax.all_to_all(small.reshape(bands, piece, channels), BANDS, 0, 0, tiled=True)
    tap_grads, bias_part = call(
        wrap(functools.partial(taps_kernel, (height, breadth, up, channels))),
        planes,
        given + [(part0, False)],
        [((planes, tok_rows * tok_cols, up * up * channels), BF, False), one],
        [pltpu.VMEM((height * breadth, channels), F32)] + room,
    )
    tap_grads = tap_grads.reshape(-1, up * up * channels)
    tap_grads, small = lax.optimization_barrier((tap_grads, small))
    product = lax.dot_general(
        tok.reshape(-1, fan), tap_grads, (((0,), (0,)), ((), ())), preferred_element_type=F32
    )
    small = small_summed(small, jnp.sum(bias_part, (0, 1)))
    parts = weight_parts(product)
    tok_grad = lax.dot_general(
        tap_grads, deconv_weight, (((1,), (1,)), ((), ())), preferred_element_type=F32
    )
    tok_grad = tok_grad.astype(BF).reshape(tokens.shape)
    parts, small, tok_grad = lax.optimization_barrier((parts, small, tok_grad))
    small = small_whole(small)
    parts, small = lax.optimization_barrier((weight_scattered(parts), small))
    weight_grad = scattered(parts, "obj")
    return (tok_grad, weight_grad) + small_results(small, conv_kernels.shape[1])


def per_device(tokens, gout, deconv_weight, deconv_bias, conv_kernels, conv_biases):
    channels = gout.shape[-1]
    sizes = [lax.axis_size(axis) for axis in ("obj", "plane", "tile")]
    fits = gout.shape[3] % 16 == 0 and gout.shape[2] % 16 == 0 and channels % 128 == 0
    fits = fits and all(size & (size - 1) == 0 and size > 1 for size in sizes)
    run = kernel_pass if fits else plain_pass
    return run(tokens, gout, deconv_weight, deconv_bias, conv_kernels, conv_biases)


def solution(mesh):
    placed = (
        P("obj", None, "plane", "tile", None),
        P("obj", None, "plane", "tile", None),
        P(),
        P(),
        P(),
        P(),
    )
    return jax.shard_map(
        per_device,
        mesh=mesh,
        in_specs=placed,
        out_specs=(
            P("obj", None, "plane", "tile", None),
            P(EVERY, None),
            P(),
            P(),
            P(),
        ),
        check_vma=False,
    )
```

```python
import functools

import jax
import jax.numpy as jnp
from jax import lax
from jax.experimental import pallas as pl
from jax.experimental.pallas import tpu as pltpu
from jax.sharding import PartitionSpec as P

BANDS = ("plane", "tile")
EVERY = ("obj", "plane", "tile")
CONV_DIMS = ("NHWC", "HWIO", "NHWC")
BF = jnp.bfloat16
F32 = jnp.float32


def shifted(array, axis, step):
    size = lax.axis_size(axis)
    pairs = [(i, i + step) for i in range(size) if 0 <= i + step < size]
    return lax.ppermute(array, axis, pairs)


def grow_dim(tok, grad, axis, dim, tok_rim, grad_rim):
    planes, lanes = tok.shape[0], grad.shape[-1]

    def cut(array, rim, last):
        length = array.shape[dim]
        start = length - rim if last else 0
        return lax.slice_in_dim(array, start, start + rim, axis=dim)

    def pack(last):
        parts = [cut(tok, tok_rim, last), cut(grad, grad_rim, last)]
        return jnp.concatenate([part.reshape(planes, -1, lanes) for part in parts], 1)

    def unpack(packed):
        shapes = [cut(tok, tok_rim, False).shape, cut(grad, grad_rim, False).shape]
        rows = shapes[0][1] * shapes[0][2] * shapes[0][3] // lanes
        return packed[:, :rows].reshape(shapes[0]), packed[:, rows:].reshape(shapes[1])

    before = unpack(shifted(pack(True), axis, 1))
    after = unpack(shifted(pack(False), axis, -1))
    return [
        jnp.concatenate([low, mid, high], axis=dim)
        for low, mid, high in zip(before, (tok, grad), after)
    ]


def band_sums(rows, cols):
    height = rows.shape[1]

    def joined(own, other, axis, step):
        upper = (lax.axis_index(axis) & step) != 0
        return jnp.where(
            upper, jnp.concatenate([other, own], 1), jnp.concatenate([own, other], 1)
        )

    rows, cols = rows.astype(BF), cols.astype(BF)
    for axis in ("tile", "plane"):
        size, step = lax.axis_size(axis), 1
        while step < size:
            height = rows.shape[1]
            other = lax.ppermute(
                jnp.concatenate([rows, cols], 1), axis, [(i, i ^ step) for i in range(size)]
            )
            other_rows, other_cols = other[:, :height], other[:, height:]
            if axis == "tile":
                rows = (rows.astype(F32) + other_rows.astype(F32)).astype(BF)
                cols = joined(cols, other_cols, axis, step)
            else:
                rows = joined(rows, other_rows, axis, step)
                cols = (cols.astype(F32) + other_cols.astype(F32)).astype(BF)
            step *= 2
    return rows.astype(F32), cols.astype(F32)


def spread(row_sum, col_sum, extent, ring, row_start, col_start, height, breadth):
    planes, _, channels = row_sum.shape
    rows = row_sum.reshape(planes // 3, 3, extent, channels) / extent
    cols = col_sum.reshape(planes // 3, 3, extent, channels) / extent
    row_ctx = jnp.stack([rows[:, 1], rows[:, 0], cols[:, 0]], 1)
    col_ctx = jnp.stack([rows[:, 2], cols[:, 2], cols[:, 1]], 1)

    def band(ctx, start, length):
        ctx = jnp.pad(ctx, ((0, 0), (0, 0), (ring, ring), (0, 0)))
        ctx = lax.dynamic_slice_in_dim(ctx, start, length + 2 * ring, 2)
        return ctx.reshape(planes, length + 2 * ring, channels)

    row_band = band(row_ctx, row_start, height)
    col_band = band(col_ctx, col_start, breadth)
    return row_band[:, :, None, :] + col_band[:, None, :, :]


def inside(ring, extent, row_start, col_start, height, breadth):
    row = row_start - ring + lax.iota(jnp.int32, height + 2 * ring)
    col = col_start - ring + lax.iota(jnp.int32, breadth + 2 * ring)
    row_ok = (row >= 0) & (row < extent)
    col_ok = (col >= 0) & (col < extent)
    return (row_ok[:, None] & col_ok[None, :])[None, :, :, None]


def conv(padded, kernel):
    return lax.conv_general_dilated(
        padded, kernel, (1, 1), "VALID", dimension_numbers=CONV_DIMS, preferred_element_type=F32
    )


def kernel_gradient(padded, grad):
    return lax.conv_general_dilated(
        padded,
        grad,
        (1, 1),
        "VALID",
        dimension_numbers=("CHWN", "IHWO", "HWNC"),
        preferred_element_type=F32,
    )


def trim(array, ring):
    return array[:, ring:-ring, ring:-ring, :]


def slope(pre):
    sig = jax.nn.sigmoid(pre)
    return sig * (1.0 + pre * (1.0 - sig))


def scattered(parts, axes):
    return jnp.sum(lax.all_to_all(parts, axes, 0, 0, tiled=True).astype(F32), 0)


def scatter_all(blocks, sizes):
    objs, bands = sizes
    blocks = blocks.astype(BF).reshape((objs, bands) + blocks.shape[1:])
    blocks = jnp.moveaxis(blocks, 1, 0)
    part = scattered(blocks, BANDS).astype(BF)
    return scattered(part, "obj")


def call(kernel, planes, ins, outs, scratch=(), flops=0):
    def spec(shape, kind):
        rest = (0,) * (len(shape) - 1)
        if kind is True:
            return pl.BlockSpec(shape, lambda p: (0,) + rest)
        if kind == "copies":
            return pl.BlockSpec(
                (shape[0], None) + shape[2:], lambda p: (0, p) + (0,) * (len(shape) - 2)
            )
        if kind is False:
            return pl.BlockSpec((None,) + shape[1:], lambda p: (p,) + rest)
        first, count = kind
        if count < 0:
            return pl.BlockSpec((None,) + shape[1:], lambda p: (p + first,) + rest)
        return pl.BlockSpec(
            (None,) + shape[1:], lambda p: (jnp.clip(p - first, 0, count - 1),) + rest
        )

    moved = sum(a.size * a.dtype.itemsize for a, _ in ins)
    return pl.pallas_call(
        kernel,
        grid=(planes,),
        in_specs=[spec(a.shape, kind) for a, kind in ins],
        out_specs=[spec(shape, kind) for shape, _, kind in outs],
        out_shape=[jax.ShapeDtypeStruct(shape, dtype) for shape, dtype, _ in outs],
        scratch_shapes=list(scratch),
        compiler_params=pltpu.CompilerParams(
            dimension_semantics=("arbitrary",), vmem_limit_bytes=60 << 20
        ),
        cost_estimate=pl.CostEstimate(
            flops=flops * planes, bytes_accessed=2 * moved, transcendentals=0
        ),
    )(*[a for a, _ in ins])


def inside_limits(ring, extent, height, breadth, width):
    row_start = lax.axis_index("plane") * height
    col_start = lax.axis_index("tile") * breadth
    edge = (width - breadth) // 2
    column = lax.broadcasted_iota(jnp.int32, (width, 128), 0) - edge
    ok = (column >= -ring) & (column < breadth + ring)
    ok = ok & (col_start + column >= 0) & (col_start + column < extent)
    ones = jnp.where(ok, 1.0, 0.0)

    def limit(r):
        row = row_start + r - ring
        return jnp.where((row >= 0) & (row < extent), 0.5, 2.0)

    return ones, limit


def span(row, width, rows=1):
    return pl.ds(pl.multiple_of(row * width, 16), rows * width)


def span8(start, size):
    return pl.ds(pl.multiple_of(start, 8), size)


def loop(rows, body, carry=None, unroll=4):
    return lax.fori_loop(0, rows, body, carry, unroll=unroll)


def convolve_rows(
    src, base, kernel_ref, prod, pair, rows_out, width, chunks, finish, carry, flipped=False
):
    step = rows_out // chunks
    pairs = step // 2
    size = pairs * width
    order = (2, 1, 0) if flipped else (0, 1, 2)
    channels = kernel_ref.shape[0] // 3
    side = 3 * channels

    @pl.when(pl.program_id(0) == 0)
    def _():
        pair[...] = jnp.zeros(pair.shape, BF)
        for row in range(2):
            for tap, dy in enumerate(order):
                at = (row + dy) * channels
                pair[at : at + channels, row * side : (row + 1) * side] = kernel_ref[
                    tap * channels : (tap + 1) * channels, :
                ]

    def chunk(index, carry):
        start = base + index * step

        def lane(j):
            block = src[span(start + j // 2 * 2, width, step), :]
            block = block.reshape(pairs, 2 * width, channels)
            return block[:, j % 2 * width : (j % 2 + 1) * width].reshape(size, channels)

        lhs = jnp.concatenate([lane(j) for j in range(4)], 1)
        prod[pl.ds(8, size), :] = jnp.dot(lhs, pair[...], preferred_element_type=F32)
        first, _, last = order

        def rows(q, carry):
            view = prod.at[span8(q * width, width + 16), :]
            for row in range(2):
                at = row * side
                value = (
                    view[7 + first : 7 + first + width, at : at + channels]
                    + view[8 : 8 + width, at + channels : at + 2 * channels]
                    + view[7 + last : 7 + last + width, at + 2 * channels : at + side]
                )
                carry = finish(index * step + 2 * q + row, value, carry)
            return carry

        return loop(pairs, rows, carry, unroll=2)

    return lax.fori_loop(0, chunks, chunk, carry)


def send_sums(sums, copies_ref):
    for copy in range(copies_ref.shape[0]):
        copies_ref[copy] = sums[...].astype(BF)


def place_row(rows, r, slot, center, left_ref, right_ref):
    side = left_ref.shape[0] // rows // 2
    at = span8((2 * r + slot) * side, side)
    return jnp.concatenate([left_ref[at, :], center, right_ref[at, :]], 0)


def place_rows(rows, breadth, slot, refs, put):
    own_ref, above_ref, below_ref, left_ref, right_ref = refs

    def one(r, ref, at):
        center = ref[at, :].astype(F32)
        put(r, place_row(rows, r, slot, center, left_ref, right_ref))

    for r in range(2):
        at = (2 * slot + r) * breadth
        one(r, above_ref, slice(at, at + breadth))
        one(rows - 2 + r, below_ref, slice(at, at + breadth))

    def inner(r, carry):
        one(r + 2, own_ref, span(r, breadth))
        return carry

    loop(rows - 4, inner, 0)


def upsample_kernel(
    dims, tok_ref, grad_ref, weight_ref,
    raw_ref, copies_ref, first_ref, last_ref, bias_ref, sums,
):
    tok_rows, tok_cols, up, height, breadth, channels = dims
    cut = up * channels
    for a in range(up):
        weight = weight_ref[:, a * cut : (a + 1) * cut]
        prod = jnp.dot(tok_ref[...], weight, preferred_element_type=F32)
        for b in range(up):
            for i in range(tok_rows):
                raw_ref[pl.ds((up * i + a) * breadth + b, tok_cols, stride=up), :] = prod[
                    i * tok_cols : (i + 1) * tok_cols, b * channels : (b + 1) * channels
                ]

    def add(r, total):
        own = raw_ref[span(r, breadth), :]
        sums[pl.ds(r, 1), :] = jnp.sum(own, 0, keepdims=True)
        total, bias = total
        return total + own, bias + grad_ref[span(r, breadth), :].astype(F32)

    zero = jnp.zeros((breadth, channels), F32)
    total, bias = loop(height, add, (zero, zero))
    sums[pl.ds(height, breadth), :] = total
    bias_ref[...] = jnp.sum(bias, 0, keepdims=True)
    send_sums(sums, copies_ref)
    rim = 2 * breadth
    tail = slice((height - 2) * breadth, height * breadth)
    for ref, at in ((first_ref, slice(0, rim)), (last_ref, tail)):
        ref[:rim, :] = grad_ref[at, :]
        ref[rim:, :] = raw_ref[at, :].astype(BF)


def forward_kernel(
    dims, extent, row_ref, col_ref, own_ref, above_ref, below_ref, left_ref, right_ref, kernel_ref,
    act_ref, slope_ref, next_ref, copies_ref, raw_ref, prod, pair, sums_ref, mask,
):
    height, breadth, width = dims
    mask[...], limit = inside_limits(2, extent, height, breadth, width)
    edge = (width - breadth) // 2

    def activate(r, value):
        raw_ref[span(r, width), :] = value
        pre = value + row_ref[pl.ds(r, 1), :] + col_ref[...]
        sig = 0.5 * jnp.tanh(0.5 * pre) + 0.5
        ok = mask[...] > limit(r)
        act = pre * sig
        act_ref[span(r, width), :] = jnp.where(ok, act, 0.0).astype(BF)
        slope_ref[span(r, width), :] = (sig + act * (1.0 - sig)).astype(BF)

    refs = (own_ref, above_ref, below_ref, left_ref, right_ref)
    place_rows(height + 4, breadth, 1, refs, activate)
    zero = jnp.zeros((breadth, sums_ref.shape[1]), F32)

    def finish(r, value, total):
        value = raw_ref[span(r + 1, width), :] + value
        next_ref[span(r, width), :] = value.astype(BF)
        own = value[edge : edge + breadth]
        inner = (r >= 1) & (r <= height)

        @pl.when(inner)
        def _():
            sums_ref[pl.ds(r - 1, 1), :] = jnp.sum(own, 0, keepdims=True)

        return total + jnp.where(inner, own, 0.0)

    sums_ref[pl.ds(height, breadth), :] = convolve_rows(
        act_ref, 0, kernel_ref, prod, pair, height + 2, width, 1, finish, zero
    )
    send_sums(sums_ref, copies_ref)


def adjoint_kernel(
    dims, own_ref, above_ref, below_ref, left_ref, right_ref, kernel_ref, wide_ref, out_ref, prod, pair
):
    height, breadth, width = dims

    def put(r, row):
        wide_ref[span(r, width), :] = row.astype(BF)

    refs = (own_ref, above_ref, below_ref, left_ref, right_ref)
    place_rows(height + 4, breadth, 0, refs, put)

    def finish(r, value, carry):
        out_ref[span(r, width), :] = value.astype(BF)
        return carry

    convolve_rows(wide_ref, 0, kernel_ref, prod, pair, height + 2, width, 1, finish, 0, True)


def context_kernel(dims, ring, side, parts_ref, bias_ref, row_ref, col_ref, rows, cols):
    height, breadth, _ = dims
    bands, planes = parts_ref.shape[:2]
    extent = rows.shape[1] - 16
    down, across = extent // height, extent // breadth
    rows[...] = jnp.zeros(rows.shape, F32)
    cols[...] = jnp.zeros(cols.shape, F32)
    scale = 1.0 / extent
    for first in range(0, planes, 3):
        for q in range(3):
            part = lambda p, t, at, size: parts_ref[p * across + t, first + q, at : at + size, :].astype(F32)
            for p in range(down):
                pieces = [part(p, t, 0, height) for t in range(across)]
                rows[q, 8 + p * height : 8 + (p + 1) * height, :] = scale * sum(pieces)
            for t in range(across):
                pieces = [part(p, t, height, breadth) for p in range(down)]
                cols[q, 8 + t * breadth : 8 + (t + 1) * breadth, :] = scale * sum(pieces)
        row_at = span8(lax.axis_index("plane") * height, height + 16)
        col_at = span8(lax.axis_index("tile") * breadth, breadth + 16)
        for q, (ref, other) in enumerate(((rows, 1), (rows, 0), (cols, 0))):
            view = ref.at[other, row_at, :]
            row_ref[first + q] = view[8 - ring : 8 + height + ring, :] + 2.0 * bias_ref[...]
        for q, (ref, other) in enumerate(((rows, 2), (cols, 2), (cols, 1))):
            view = ref.at[other, col_at, :]
            col_ref[first + q] = view[8 - side : 8 + breadth + side, :] + bias_ref[...]


def with_contexts(kernel, dims, ring, side):
    def body(parts_ref, bias_ref, *refs):
        row_all, col_all, rows, cols = refs[-4:]

        @pl.when(pl.program_id(0) == 0)
        def _():
            context_kernel(
                dims, ring, side, parts_ref, bias_ref, row_all, col_all, rows, cols
            )

        plane = pl.program_id(0)
        kernel(row_all.at[plane], col_all.at[plane], *refs[:-4])

    return body


def middle_kernel(
    dims, extent, half, row_ref, col_ref, hid_ref, adj_low, adj_high, grad_low, grad_high, act_ref, next_ref, copies_ref, sums_ref, mask,
):
    height, breadth, width = dims
    mask[...], limit = inside_limits(1, extent, height, breadth, width)
    low = pl.program_id(0) < half
    edge = (width - breadth) // 2

    def one(r, total):
        pre = hid_ref[span(r, width), :].astype(F32) + row_ref[pl.ds(r, 1), :] + col_ref[...]
        sig = 0.5 * jnp.tanh(0.5 * pre) + 0.5
        ok = mask[...] > limit(r)
        act = pre * sig
        act_ref[span(r, width), :] = jnp.where(ok, act, 0.0).astype(BF)
        here, after = span(r, width), span(r + 1, width)
        adj = jnp.where(low, adj_low[here, :].astype(F32), adj_high[here, :].astype(F32))
        grad = jnp.where(low, grad_low[after, :].astype(F32), grad_high[after, :].astype(F32))
        dz = adj * (sig + act * (1.0 - sig))
        next_ref[here, :] = (grad + dz).astype(BF)
        own = dz[edge : edge + breadth]
        inner = (r >= 1) & (r <= height)

        @pl.when(inner)
        def _():
            sums_ref[pl.ds(r - 1, 1), :] = jnp.sum(own, 0, keepdims=True)

        return total + jnp.where(inner, own, 0.0)

    sums_ref[pl.ds(height, breadth), :] = loop(height + 2, one, jnp.zeros((breadth, sums_ref.shape[1]), F32))
    send_sums(sums_ref, copies_ref)


def backward_kernel(
    dims, extent, row_ref, col_ref, part_ref, slope_ref, kernel_ref,
    grad_ref, next_ref, copies_ref, bias_ref, prod, pair, sums_ref, mask,
):
    height, breadth, width = dims
    mask[...], limit = inside_limits(1, extent, height, breadth, width)
    edge = (width - breadth) // 2

    def full(r):
        return part_ref[span(r, width), :].astype(F32) + row_ref[pl.ds(r, 1), :] + col_ref[...]

    def round_row(r, carry):
        ok = mask[...] > limit(r)
        grad_ref[span(r, width), :] = jnp.where(ok, full(r), 0.0).astype(BF)
        return carry

    loop(height + 2, round_row, 0)
    zero = jnp.zeros((breadth, sums_ref.shape[1]), F32)

    def finish(r, value, carry):
        total, bias = carry
        dz = value * slope_ref[span(r + 2, width), :].astype(F32)
        own = dz[edge : edge + breadth]
        grad = full(r + 1)[edge : edge + breadth]
        sums_ref[pl.ds(r, 1), :] = jnp.sum(own, 0, keepdims=True)
        next_ref[pl.ds(pl.multiple_of(r * breadth, 16), breadth), :] = (grad + own).astype(BF)
        return total + own, bias + grad

    total, bias = convolve_rows(
        grad_ref, 0, kernel_ref, prod, pair, height, width, 1, finish, (zero, zero), True
    )
    sums_ref[pl.ds(height, breadth), :] = total
    send_sums(sums_ref, copies_ref)
    bias_ref[...] = jnp.sum(bias, 0, keepdims=True)


def taps_kernel(dims, row_ref, col_ref, part_ref, tap_ref, bias_ref, full):
    height, breadth, up, channels = dims

    def one(r, total):
        at = pl.ds(pl.multiple_of(r * breadth, 16), breadth)
        value = part_ref[at, :].astype(F32) + row_ref[pl.ds(r, 1), :] + col_ref[...]
        full[at, :] = value
        return total + value

    total = loop(height, one, jnp.zeros(col_ref.shape, F32))
    bias_ref[...] = jnp.sum(total, 0, keepdims=True)
    tok_cols = breadth // up
    for i in range(height // up):
        for a in range(up):
            for b in range(up):
                piece = full[pl.ds((up * i + a) * breadth + b, tok_cols, stride=up), :]
                tap = a * up + b
                tap_ref[
                    i * tok_cols : (i + 1) * tok_cols, tap * channels : (tap + 1) * channels
                ] = piece.astype(BF)


def kernel_grad_kernel(dims, act_base, grad_base, act_ref, grad_ref, *refs):
    more, (rounded_ref, wide, moved, out_ref) = refs[:-4], refs[-4:]

    height, breadth, width = dims
    edge = (width - breadth) // 2
    channels = act_ref.shape[1]
    column = lax.broadcasted_iota(jnp.int32, (width, channels), 0)
    ok = (column >= edge) & (column < edge + breadth)
    wide[pl.ds(0, 8), :] = jnp.zeros((8, channels), F32)
    wide[pl.ds(8 + height * width, 8), :] = jnp.zeros((8, channels), F32)

    def fill(r, carry):
        if grad_base is None:
            value = grad_ref[span(r, breadth), :].astype(F32)
            rim = jnp.zeros((edge, channels), F32)
            value = jnp.concatenate([rim, value, rim], 0)
        else:
            value = jnp.where(ok, grad_ref[span(r + grad_base, width), :].astype(F32), 0.0)
        wide[span8(r * width + 8, width), :] = value
        return carry

    loop(height, fill, 0)

    def move(r, carry):
        view = wide.at[span8(r * width, width + 16), :]
        for dx in range(3):
            moved[span(r, width), dx * channels : (dx + 1) * channels] = view[
                9 - dx : 9 - dx + width, :
            ].astype(BF)
        return carry

    loop(height, move, 0)

    @pl.when(pl.program_id(0) == 0)
    def _():
        out_ref[...] = jnp.zeros(out_ref.shape, F32)

    chunks = 2
    step = height // chunks

    def chunk(index, carry):
        start = index * step
        lhs = jnp.concatenate(
            [act_ref[span(start + act_base + dy, width, step), :] for dy in range(3)], 1
        )
        result = lax.dot_general(
            lhs,
            moved[span(start, width, step), :],
            (((0,), (0,)), ((), ())),
            preferred_element_type=F32,
        )
        for tap in range(9):
            dy, dx = divmod(tap, 3)
            out_ref[tap * channels : (tap + 1) * channels, :] += result[
                dy * channels : (dy + 1) * channels, dx * channels : (dx + 1) * channels
            ]
        return carry

    lax.fori_loop(0, chunks, chunk, 0)

    @pl.when(pl.program_id(0) == pl.num_programs(0) - 1)
    def _():
        size = out_ref.shape[0]
        rounded_ref[:size, :] = out_ref[...].astype(BF)
        if more:
            other_ref, bias0_ref, bias1_ref = more
            rounded_ref[size : 2 * size, :] = other_ref[...]
            tail = rounded_ref.shape[0] - 2 * size
            row = lax.broadcasted_iota(jnp.int32, (tail, channels), 0)
            bias0 = jnp.sum(bias0_ref[...], 0)
            bias1 = jnp.sum(bias1_ref[...], 0)
            value = jnp.where(row == 0, bias0, jnp.where(row == 1, bias1, 0.0))
            rounded_ref[2 * size :, :] = value.astype(BF)


def plain_pass(tokens, gout, deconv_weight, deconv_bias, conv_kernels, conv_biases):
    objects, _, tok_rows, tok_cols, fan = tokens.shape
    _, _, height, breadth, channels = gout.shape
    planes = 3 * objects
    up = height // tok_rows
    extent = height * lax.axis_size("plane")
    row_start = lax.axis_index("plane") * height
    col_start = lax.axis_index("tile") * breadth
    place = (extent, row_start, col_start, height, breadth)
    ctx_place = (row_start, col_start, height, breadth)

    tok = tokens.reshape(planes, tok_rows, tok_cols, fan)
    grad_top = gout.reshape(planes, height, breadth, channels)
    tok_wide, grad_wide = grow_dim(tok, grad_top, "plane", 1, 1, 2)
    tok_wide, grad_wide = grow_dim(tok_wide, grad_wide, "tile", 2, 1, 2)

    taps = conv_kernels.reshape(2, 3, 3, channels, channels)
    back = taps[:, ::-1, ::-1].transpose(0, 1, 2, 4, 3)

    raw = jnp.dot(tok_wide.reshape(-1, fan), deconv_weight, preferred_element_type=F32)
    raw = raw.reshape(planes, tok_rows + 2, tok_cols + 2, up, up, channels)
    raw = raw.transpose(0, 1, 3, 2, 4, 5)
    raw = raw.reshape(planes, up * (tok_rows + 2), up * (tok_cols + 2), channels)
    raw = trim(raw, up - 2)

    own = trim(raw, 2)
    row0, col0 = band_sums(jnp.sum(own, 2), jnp.sum(own, 1))
    bias = deconv_bias
    pre0 = raw + bias + spread(
        row0 + extent * bias, col0 + extent * bias, extent, 2, *ctx_place
    )
    act0 = jnp.where(inside(2, *place), jax.nn.silu(pre0), 0.0).astype(BF)
    step0 = conv(act0, taps[0])

    own = trim(step0, 1)
    row1, col1 = band_sums(jnp.sum(own, 2), jnp.sum(own, 1))
    bias = deconv_bias + conv_biases[0]
    pre1 = trim(raw, 1) + step0 + bias + spread(
        row0 + row1 + extent * bias, col0 + col1 + extent * bias, extent, 1, *ctx_place
    )
    ok1 = inside(1, *place)
    act1 = jnp.where(ok1, jax.nn.silu(pre1), 0.0).astype(BF)

    dz1 = conv(grad_wide, back[1]) * slope(pre1)
    own = trim(dz1, 1)
    drow1, dcol1 = band_sums(jnp.sum(own, 2), jnp.sum(own, 1))
    kernel1 = kernel_gradient(act1, grad_top)
    cbias1 = jnp.sum(grad_top.astype(F32), (0, 1, 2))
    grad1 = trim(grad_wide, 1).astype(F32) + dz1 + spread(drow1, dcol1, extent, 1, *ctx_place)
    gb1 = jnp.where(ok1, grad1, 0.0).astype(BF)
    own1 = trim(grad1, 1)
    cbias0 = jnp.sum(own1, (0, 1, 2))

    dz0 = conv(gb1, back[0]) * slope(trim(pre0, 2))
    drow0, dcol0 = band_sums(jnp.sum(dz0, 2), jnp.sum(dz0, 1))
    kernel0 = kernel_gradient(trim(act0, 1), trim(gb1, 1))
    grad0 = own1 + dz0 + spread(drow0, dcol0, extent, 0, *ctx_place)
    bias_part = jnp.sum(grad0, (0, 1, 2))

    gb0 = grad0.astype(BF).reshape(planes, tok_rows, up, tok_cols, up, channels)
    tap_grads = gb0.transpose(0, 1, 3, 2, 4, 5).reshape(-1, up * up * channels)
    tok_grad = lax.dot_general(
        tap_grads, deconv_weight, (((1,), (1,)), ((), ())), preferred_element_type=F32
    )
    tok_grad = tok_grad.astype(BF).reshape(tokens.shape)
    weight_part = lax.dot_general(
        tok.reshape(-1, fan), tap_grads, (((0,), (0,)), ((), ())), preferred_element_type=F32
    )
    small = jnp.concatenate(
        [kernel0.reshape(-1, channels), kernel1.reshape(-1, channels)]
        + [v.reshape(1, channels) for v in (cbias0, cbias1)],
        0,
    )
    bands = lax.axis_size(BANDS)
    piece = -(-small.shape[0] // bands)
    piece += -piece % 16
    small = jnp.pad(small, ((0, piece * bands - small.shape[0]), (0, 0))).astype(BF)
    small = lax.all_to_all(small.reshape(bands, piece, channels), BANDS, 0, 0, tiled=True)
    small = lax.all_to_all(small_copies(small, bias_part), "obj", 0, 0, tiled=True)
    small = small_whole(small)
    bands = lax.axis_size("plane") * lax.axis_size("tile")
    total = lax.axis_size("obj") * bands
    weight_grad = scatter_all(
        weight_part.reshape(total, fan // total, -1), (lax.axis_size("obj"), bands)
    )
    return (tok_grad, weight_grad) + small_results(small, conv_kernels.shape[1])


def sent_to_all(array, axes):
    copies = jnp.broadcast_to(array[None], (lax.axis_size(axes),) + array.shape)
    return lax.all_to_all(copies, axes, 0, 0, tiled=True)


def small_copies(parts, bias_part):
    piece = jnp.sum(parts.astype(F32), 0)
    tail = jnp.pad(bias_part[None], ((0, 15), (0, 0)))
    piece = jnp.concatenate([piece, tail], 0).astype(BF)
    return jnp.broadcast_to(piece[None], (lax.axis_size("obj"),) + piece.shape)


def small_whole(parts):
    return sent_to_all(jnp.sum(parts.astype(F32), 0).astype(BF), BANDS)


def small_results(parts, per_kernel):
    channels = parts.shape[-1]
    small = parts[:, :-16].reshape(-1, channels).astype(F32)
    bias = jnp.sum(parts[:, -16].astype(F32), 0)
    kernel_grads = small[: 2 * per_kernel].reshape(2, per_kernel, channels)
    return (bias, kernel_grads, small[2 * per_kernel : 2 * per_kernel + 2])


def bits_of(size):
    steps = []
    while size > 1:
        size //= 2
        steps.append(size)
    return steps


def parted(parts, dim, axis, step):
    upper = ((lax.axis_index(axis) // step) % 2).astype(jnp.int32)
    mine = lax.dynamic_slice_in_dim(parts, upper, 1, dim)
    return mine, lax.dynamic_slice_in_dim(parts, 1 - upper, 1, dim)


def joined(mine, theirs, axis, step):
    size = lax.axis_size(axis)
    other = lax.ppermute(theirs, axis, [(i, i ^ step) for i in range(size)])
    return (mine.astype(F32) + other.astype(F32)).astype(BF)


def halved(parts, dim, axis, step):
    return joined(*parted(parts, dim, axis, step), axis, step)


def near_step():
    return ("plane", 1), 1 + len(bits_of(lax.axis_size("plane"))) - 1


def weight_parts(product):
    fan, columns = product.shape
    objs = lax.axis_size("obj")
    bits = len(bits_of(lax.axis_size("plane"))) + len(bits_of(lax.axis_size("tile")))
    shape = (objs,) + (2,) * bits + (fan // (objs * 2**bits), columns)
    step, dim = near_step()
    return halved(product.astype(BF).reshape(shape), dim, *step)


def weight_scattered(parts, beside):
    objs = parts.shape[0]
    steps = [("plane", s) for s in bits_of(lax.axis_size("plane"))]
    steps += [("tile", s) for s in bits_of(lax.axis_size("tile"))]
    rest = [(i + 1, step) for i, step in enumerate(steps) if i + 1 != near_step()[1]]
    streams = [parts[: objs // 2], parts[objs // 2 :]]
    for turn, pair in enumerate(zip(rest, reversed(rest))):
        cut = [parted(stream, dim, *step) for stream, (dim, step) in zip(streams, pair)]
        if turn == 0:
            cut, beside = lax.optimization_barrier((cut, beside))
        streams = [joined(*halves, *step) for halves, (_, step) in zip(cut, pair)]
    return beside, jnp.concatenate(streams, 0).reshape(objs, *parts.shape[-2:])


def kernel_pass(tokens, gout, deconv_weight, deconv_bias, conv_kernels, conv_biases):
    objects, _, tok_rows, tok_cols, fan = tokens.shape
    _, _, height, breadth, channels = gout.shape
    planes = 3 * objects
    up = height // tok_rows
    edge = 8
    width = breadth + 2 * edge
    extent = height * lax.axis_size("plane")
    row_start = lax.axis_index("plane") * height
    col_start = lax.axis_index("tile") * breadth
    dims = (height, breadth, width)

    tok = tokens.reshape(planes, tok_rows, tok_cols, fan)
    grad_top = gout.reshape(planes, height, breadth, channels)
    flat_tok = lambda array: array.reshape(planes, -1, fan)
    flat_grad = lambda array: array.reshape(planes, -1, channels)

    def columns_beside(bands_of, last):
        def cut(parts):
            cells = [p[:, :, -2:] if last else p[:, :, :2] for p in parts]
            cells = lax.optimization_barrier(cells)
            return jnp.concatenate([c.astype(BF) for c in cells], 1)

        rim = shifted(jnp.stack([cut(parts) for parts in bands_of], 2), "tile", 1 if last else -1)
        room = (edge - 2, 0) if last else (0, edge - 2)
        return flat_grad(jnp.pad(rim, ((0, 0),) * 3 + (room, (0, 0))).astype(F32))

    taps = conv_kernels.reshape(2, 3, 3, channels, channels)
    side = 3 * channels
    ahead = taps[0].transpose(0, 2, 1, 3).reshape(side, side)
    back = taps.transpose(0, 1, 4, 2, 3).reshape(2, side, side)

    flat = lambda rows: (planes, rows * width, channels)
    bands = lax.axis_size(BANDS)
    copies = ((bands, planes, height + breadth, channels), BF, "copies")
    sums = pltpu.VMEM((height + breadth, channels), F32)
    one = ((planes, 1, channels), F32, False)
    prod = lambda rows: [
        pltpu.VMEM((rows // 2 * width + 16, 2 * side), F32),
        pltpu.VMEM((4 * channels, 2 * side), BF),
    ]
    conv_flops = lambda rows: 2 * rows * width * side * side
    mask = pltpu.VMEM((width, channels), F32)

    def contexts(parts, rim, pad, bias, beside):
        parts = lax.all_to_all(parts, BANDS, 0, 0, tiled=True)
        parts, beside = lax.optimization_barrier((parts, beside))
        room = [
            pltpu.VMEM((planes, height + 2 * rim, channels), F32),
            pltpu.VMEM((planes, breadth + 2 * pad, channels), F32),
        ] + [pltpu.VMEM((3, extent + 16, channels), F32)] * 2
        given = [(parts, True), (bias.reshape(1, channels), True)]
        return given, room, lambda kernel: with_contexts(kernel, dims, rim, pad), beside

    rim_rows = ((planes, 4 * breadth, channels), BF, False)
    raw, parts, first, last, cbias1 = call(
        functools.partial(upsample_kernel, (tok_rows, tok_cols, up, height, breadth, channels)),
        planes,
        [(flat_tok(tok), False), (flat_grad(grad_top), False), (deconv_weight, True)],
        [((planes, height * breadth, channels), F32, False), copies, rim_rows, rim_rows, one],
        [sums],
        flops=2 * tok_rows * tok_cols * fan * up * up * channels,
    )
    half = planes // 2
    above, below = shifted(last, "plane", 1), shifted(first, "plane", -1)
    slots = lambda array: array.reshape(planes, 2, 2, breadth, channels)
    beyond = (slots(above), slots(below))
    both = [
        (beyond[0][:, slot], cells, beyond[1][:, slot])
        for slot, cells in enumerate((grad_top, raw.reshape(grad_top.shape)))
    ]
    left, right = columns_beside(both, True), columns_beside(both, False)
    parts, left, right = lax.optimization_barrier((parts, left, right))

    def adjoint_of(first, count):
        kind = (first, -count)
        return call(
            functools.partial(adjoint_kernel, dims),
            count,
            [(flat_grad(grad_top), kind)]
            + [(array, kind) for array in (above, below, left, right)]
            + [(back[1], True)],
            [
                ((count, (height + 4) * width, channels), BF, False),
                ((count, (height + 2) * width, channels), BF, False),
            ],
            prod(height + 2),
            conv_flops(height + 2),
        )

    low = adjoint_of(0, half)
    given, room, wrap, low = contexts(parts, 2, edge, deconv_bias, low)
    act0, slope0, hidden, parts = call(
        wrap(functools.partial(forward_kernel, dims, extent)),
        planes,
        given
        + [(raw, False)]
        + [(array, False) for array in (above, below, left, right)]
        + [(ahead, True)],
        [(flat(height + 4), BF, False)] * 2 + [(flat(height + 2), BF, False), copies],
        [pltpu.VMEM(flat(height + 4)[1:], F32), *prod(height + 2), sums, mask]
        + room,
        conv_flops(height + 2),
    )
    high = adjoint_of(half, planes - half)
    given, room, wrap, high = contexts(parts, 1, edge, deconv_bias + conv_biases[0], high)
    act1, part1, parts = call(
        wrap(functools.partial(middle_kernel, dims, extent, half)),
        planes,
        given
        + [(hidden, False)]
        + [(low[1], (0, half)), (high[1], (half, planes - half))]
        + [(low[0], (0, half)), (high[0], (half, planes - half))],
        [(flat(height + 2), BF, False), (flat(height + 2), BF, False), copies],
        [sums, mask] + room,
    )

    def kernel_gradient_of(act, grad, act_base, grad_base, more=(), rows=9 * channels):
        (result,) = call(
            functools.partial(kernel_grad_kernel, dims, act_base, grad_base),
            planes,
            [(act, False), (grad, False)] + [(array, True) for array in more],
            [((rows, channels), BF, True)],
            [
                pltpu.VMEM((height * width + 16, channels), F32),
                pltpu.VMEM((height * width, side), BF),
                pltpu.VMEM((9 * channels, channels), F32),
            ],
            2 * height * width * side * side,
        )
        return result

    none = jnp.zeros((channels,), F32)
    kernel1 = kernel_gradient_of(act1, flat_grad(grad_top), 0, None)
    given, room, wrap, kernel1 = contexts(parts, 1, edge, none, kernel1)
    gb1, part0, parts, cbias0 = call(
        wrap(functools.partial(backward_kernel, dims, extent)),
        planes,
        given + [(part1, False), (slope0, False), (back[0], True)],
        [(flat(height + 2), BF, False), ((planes, height * breadth, channels), BF, False)]
        + [copies, one],
        [*prod(height), sums, mask] + room,
        conv_flops(height),
    )
    piece = -(-(18 * channels + 2) // bands)
    piece += -piece % 16
    more = (kernel1, cbias0, cbias1)
    small = kernel_gradient_of(act0, gb1, 1, 1, more, piece * bands)
    given, room, wrap, small = contexts(parts, 0, 0, none, small)
    small = lax.all_to_all(small.reshape(bands, piece, channels), BANDS, 0, 0, tiled=True)
    tap_grads, bias_part = call(
        wrap(functools.partial(taps_kernel, (height, breadth, up, channels))),
        planes,
        given + [(part0, False)],
        [((planes, tok_rows * tok_cols, up * up * channels), BF, False), one],
        [pltpu.VMEM((height * breadth, channels), F32)] + room,
    )
    tap_grads = tap_grads.reshape(-1, up * up * channels)
    copies = small_copies(small, jnp.sum(bias_part, (0, 1)))
    tap_grads, copies = lax.optimization_barrier((tap_grads, copies))
    small = lax.all_to_all(copies, "obj", 0, 0, tiled=True)
    product = lax.dot_general(
        tok.reshape(-1, fan), tap_grads, (((0,), (0,)), ((), ())), preferred_element_type=F32
    )
    parts = weight_parts(product)
    parts, small = lax.optimization_barrier((parts, small))
    small = small_whole(small)
    tap_grads, parts = weight_scattered(parts, tap_grads)
    tok_grad = lax.dot_general(
        tap_grads, deconv_weight, (((1,), (1,)), ((), ())), preferred_element_type=F32
    )
    tok_grad = tok_grad.astype(BF).reshape(tokens.shape)
    parts, small, tok_grad = lax.optimization_barrier((parts, small, tok_grad))
    weight_grad = scattered(parts, "obj")
    return (tok_grad, weight_grad) + small_results(small, conv_kernels.shape[1])


def per_device(tokens, gout, deconv_weight, deconv_bias, conv_kernels, conv_biases):
    channels = gout.shape[-1]
    sizes = [lax.axis_size(axis) for axis in ("obj", "plane", "tile")]
    fits = gout.shape[3] % 16 == 0 and gout.shape[2] % 16 == 0 and channels % 128 == 0
    fits = fits and all(size & (size - 1) == 0 and size > 1 for size in sizes)
    run = kernel_pass if fits else plain_pass
    return run(tokens, gout, deconv_weight, deconv_bias, conv_kernels, conv_biases)


def solution(mesh):
    placed = (
        P("obj", None, "plane", "tile", None),
        P("obj", None, "plane", "tile", None),
        P(),
        P(),
        P(),
        P(),
    )
    return jax.shard_map(
        per_device,
        mesh=mesh,
        in_specs=placed,
        out_specs=(
            P("obj", None, "plane", "tile", None),
            P(EVERY, None),
            P(),
            P(),
            P(),
        ),
        check_vma=False,
    )
```
